32 devices in a mesh: gx: 8 (over y, x, core), gy: 4 (over z).
Axes of the slice: x: 2, y: 2, z: 4, core: 2. Of those that a mesh axis runs over, the one named last changes fastest.
Arguments:
- slab_tokens: bfloat16 [16, 8, 16, 512], P('gx', None, 'gy'), may hold values from -6 to 6
- cotangent: bfloat16 [16, 8, 16, 512], P('gx', 'gy'), may hold values from -6 to 6
- w_qkv: bfloat16 [1536, 512], replicated, may hold values from -1 to 1
- w_out: bfloat16 [512, 512], replicated, may hold values from -0.75 to 0.75
- logit_scale: float32 [8], replicated, may hold values from 1 to 400
Outputs:
- output: bfloat16 [16, 8, 16, 512], P('gx', 'gy')
- grad_input: bfloat16 [16, 8, 16, 512], P('gx', None, 'gy')
- grad_weights: float32 [2048, 512], P(('gx', 'gy'))
The draws below stay inside these ranges and needn't reach their ends.
All inputs are finite; a program needn't handle non-finite values.
Results may differ from the reference program's by a relative error of at most 0.011.
The reference program's roundings to bfloat16 on the way count: a program that leaves them out, or rounds other values in their place, can miss the bound.
Values may be sent and summed in bfloat16 or wider, within the bound.
No kernel may reach another device: no remote copies, remote signals or barrier semaphores. Data moves between devices by JAX's collectives and lax.ppermute only.
A program may use at most 128 MiB of HBM per device.

```python
import math
import jax
import jax.numpy as jnp
from jax import lax

D = 512
HEADS = 8
HEAD_DIM = 64
NX = 16
NY = 8
NZ = 16
TOKENS = 2048


def draw_slab_tokens(key, part):
    extent = (NX, NY, NZ, D)
    values = jax.random.normal(key, extent, jnp.float32)
    return jnp.clip(values, -6.0, 6.0).astype(jnp.bfloat16)


def draw_w_qkv(key, part):
    bound = 4.0 / math.sqrt(D)
    key_first = jax.random.fold_in(key, 0)
    base = jax.random.normal(key_first, (3 * D, D), jnp.float32) / math.sqrt(D)
    return jnp.clip(base, -bound, bound).astype(jnp.bfloat16)


def draw_logit_scale(key, part):
    lowest = 1.0
    highest = 16.0
    return jnp.exp(jax.random.uniform(key, (HEADS,), jnp.float32, math.log(lowest), math.log(highest)))


def raised(array, own_key, source, target, blocks, factor):
    owner, partner = [(jnp.arange(array.shape[position]) // (array.shape[position] // blocks)).reshape([-1 if axis == position else 1 for axis in range(array.ndim)]) for position in (source, target)]
    chosen = jax.random.permutation(own_key, blocks)[partner]
    strong = (owner == chosen) | (owner == (partner + blocks // 2) % blocks)
    return jnp.where(strong, factor * array, array)


def shard_levels(rng, dims, pieces, least, top_value):
    def one(axis_at, shards_of):
        draws = jax.random.uniform(jax.random.fold_in(jax.random.fold_in(rng, 6), axis_at), (shards_of,), jnp.float32, least / len(pieces), top_value / len(pieces))
        return jnp.repeat(jnp.exp(draws), dims[axis_at] // shards_of).reshape((-1,) + (1,) * (len(dims) - axis_at - 1))

    factor_of = one(*pieces[0])
    for cut in pieces[1:]:
        factor_of = factor_of * one(*cut)
    return factor_of


def scatter_about(rng, dims, width, most, cuts=(), kind=jnp.bfloat16):
    result = width * jax.random.normal(rng, dims, jnp.float32)
    if cuts:
        result = result * shard_levels(rng, dims, cuts, -0.22, 0.18)
    return jnp.clip(result, -most, most).astype(kind)


def bell_draw_with(own_key, shape, deviation, most, cuts, heavy, kind=jnp.bfloat16):
    entries = deviation * jax.random.normal(own_key, shape, jnp.float32)
    if cuts:
        entries = entries * shard_levels(own_key, shape, cuts, -0.22, 0.18)
    return jnp.clip(raised(entries, jax.random.fold_in(own_key, 3), *heavy), -most, most).astype(kind)


def setup_inputs(seed: int = 0) -> dict:
    arg_keys = jax.random.split(jax.random.key(seed), 6)
    slab_tokens = draw_slab_tokens(jax.random.fold_in(arg_keys[5], 71), 0)
    cotangent = bell_draw_with(arg_keys[1], (NX, NY, NZ, D), 1.0, 6.0, ((0, 8), (1, 4)), (0, 3, 8, 2.0))
    w_qkv = draw_w_qkv(jax.random.fold_in(arg_keys[5], 71), 0)
    w_out = scatter_about(arg_keys[3], (D, D), (D // 8) ** -0.5, 0.75)
    logit_scale = draw_logit_scale(jax.random.fold_in(arg_keys[5], 71), 0)
    return {"slab_tokens": slab_tokens, "cotangent": cotangent, "w_qkv": w_qkv, "w_out": w_out, "logit_scale": logit_scale}


EPSILON = 1e-06
NEGATIVE = -1e+30
OFFSETS = tuple(((first, second, third) for first in range(3) for second in range(3) for third in range(3)))

def rms_rows(values):
    return values * lax.rsqrt(lax.optimization_barrier(jnp.mean(values * values, axis=-1, keepdims=True)) + EPSILON)

def head_split(values):
    return values.reshape(values.shape[:-1] + (HEADS, HEAD_DIM))

def project_heads(qkv_all, logit_scale):
    leading = qkv_all.shape[:-1]
    query_part = rms_rows(head_split(qkv_all[..., :D])) * (logit_scale / HEAD_DIM)[:, None]
    key_part = rms_rows(head_split(qkv_all[..., D:2 * D]))
    pairs = jnp.concatenate([key_part.reshape(leading + (D,)), qkv_all[..., 2 * D:]], axis=-1)
    return (query_part.reshape(leading + (D,)), pairs)

def offset_score(offset):

    def compute(queries, key_part):
        extent = queries.shape[:3]
        window = lax.slice(key_part, (offset[0], offset[1], offset[2], 0), (offset[0] + extent[0], offset[1] + extent[1], offset[2] + extent[2], key_part.shape[3]))
        return lax.optimization_barrier(jnp.sum(head_split(queries) * head_split(window), axis=-1))
    return jax.checkpoint(compute)

def offset_mix(offset):

    def compute(weights, value_part):
        extent = weights.shape[:3]
        window = lax.slice(value_part, (offset[0], offset[1], offset[2], 0), (offset[0] + extent[0], offset[1] + extent[1], offset[2] + extent[2], value_part.shape[3]))
        return (weights[..., None] * head_split(window)).reshape(extent + (D,))
    return jax.checkpoint(compute)

def attend(queries, kv_ext, start_x, start_y, total_x, total_y):
    extent = queries.shape[:3]
    key_part = kv_ext[..., :D]
    value_part = kv_ext[..., D:]
    pos_x = start_x + lax.iota(jnp.int32, extent[0])
    pos_y = start_y + lax.iota(jnp.int32, extent[1])
    pos_z = lax.iota(jnp.int32, extent[2])
    scores = []
    for offset in OFFSETS:
        flag_x = (pos_x + offset[0] - 1 >= 0) & (pos_x + offset[0] - 1 < total_x)
        flag_y = (pos_y + offset[1] - 1 >= 0) & (pos_y + offset[1] - 1 < total_y)
        flag_z = (pos_z + offset[2] - 1 >= 0) & (pos_z + offset[2] - 1 < extent[2])
        inside = flag_x[:, None, None, None] & flag_y[None, :, None, None] & flag_z[None, None, :, None]
        scores.append(jnp.where(inside, offset_score(offset)(queries, key_part), NEGATIVE))
    stacked = jnp.stack(scores)
    weights = jax.nn.softmax(stacked, axis=0)
    log_totals = jax.nn.logsumexp(stacked, axis=0)
    blended = jnp.zeros(extent + (D,), queries.dtype)
    for index, offset in enumerate(OFFSETS):
        blended = blended + offset_mix(offset)(weights[index], value_part)
    return (blended, log_totals)

def reference(slab_tokens, cotangent, w_qkv, w_out, logit_scale):
    size_x, size_y, size_z = slab_tokens.shape[:3]
    x_float = slab_tokens.astype(jnp.float32)
    normed_float, norm_back = jax.vjp(rms_rows, x_float)
    normed_rows = normed_float.astype(jnp.bfloat16).reshape(-1, D)
    qkv_all = jnp.dot(normed_rows, w_qkv.T, preferred_element_type=jnp.float32).reshape(size_x, size_y, size_z, 3 * D)
    (query_float, pair_float), head_back = jax.vjp(lambda qkv_arg: project_heads(qkv_arg, logit_scale), qkv_all)
    query_b = query_float.astype(jnp.bfloat16)
    pair_b = pair_float.astype(jnp.bfloat16)
    kv_ext = jnp.pad(pair_b, ((1, 1), (1, 1), (1, 1), (0, 0))).astype(jnp.float32)
    attended, attention_back, log_totals = jax.vjp(lambda query_arg, pair_arg: attend(query_arg, pair_arg, 0, 0, size_x, size_y), query_b.astype(jnp.float32), kv_ext, has_aux=True)
    attended_rows = attended.astype(jnp.bfloat16).reshape(-1, D)
    projected = jnp.dot(attended_rows, w_out.T, preferred_element_type=jnp.float32)
    output = (x_float + projected.reshape(x_float.shape)).astype(jnp.bfloat16)
    grad_rows = cotangent.reshape(-1, D)
    upstream = jnp.dot(grad_rows, w_out, preferred_element_type=jnp.float32).astype(jnp.bfloat16)
    grad_query, grad_ext = attention_back(upstream.reshape(x_float.shape).astype(jnp.float32))
    grad_kv = grad_ext[1:-1, 1:-1, 1:-1]
    grad_qkv, = head_back((grad_query, grad_kv))
    grad_qkv_b = grad_qkv.astype(jnp.bfloat16).reshape(-1, 3 * D)
    grad_normed = jnp.dot(grad_qkv_b, w_qkv, preferred_element_type=jnp.float32).reshape(x_float.shape)
    grad_norm_in, = norm_back(grad_normed)
    grad_input = (cotangent.astype(jnp.float32) + grad_norm_in).astype(jnp.bfloat16)
    factor = 1.0 / math.sqrt(TOKENS)
    grad_first = jnp.dot(grad_qkv_b.T, normed_rows, preferred_element_type=jnp.float32) * factor
    grad_second = jnp.dot(grad_rows.T, attended_rows, preferred_element_type=jnp.float32) * factor
    grad_weights = jnp.concatenate([grad_first, grad_second], axis=0)
    return (output, grad_input, grad_weights)
```

```python
import math

import jax
import jax.numpy as jnp
from jax import lax
from jax.experimental import pallas as pl
from jax.experimental.pallas import tpu as pltpu
from jax.sharding import PartitionSpec as P

D = 512
HEADS = 8
HEAD_DIM = 64
EPSILON = 1e-06
NEGATIVE = -1e30
F32 = jnp.float32
BF16 = jnp.bfloat16

NN = (((1,), (0,)), ((), ()))
NT = (((1,), (1,)), ((), ()))
TN = (((0,), (0,)), ((), ()))


def mm(a, b, dims=NN):
    return lax.dot_general(a, b, dims, preferred_element_type=F32)


def iota(shape, dim):
    return lax.broadcasted_iota(jnp.int32, shape, dim)


def head_sums(values, ones):
    high = values.astype(BF16)
    low = (values - high.astype(F32)).astype(BF16)
    return mm(high, ones) + mm(low, ones)


def select_rows(count, source_of):
    rows = iota((count, 1), 0)
    cols = iota((1, count), 1)
    return (source_of(rows) == cols).astype(F32).astype(BF16)


def main_kernel(
    pos_ref, own_ref, xl_ref, xh_ref, zl_ref, zh_ref, cot_ref, wqkv_ref, wout_ref, scale_ref,
    send_ref, out_ref, gin_ref,
    e_ref, dq_ref, dk_ref, dv_ref, att_ref,
    *, ny, n_gx, n_gy, total_x, total_z,
):
    plane = 8 * ny
    inner = 4 * ny
    qplane = 6 * ny
    tokens = 2 * inner
    yb = ny // n_gy
    for p in range(2):
        e_ref[p, 2 * ny : 6 * ny] = xl_ref[p * inner : (p + 1) * inner]
        e_ref[p + 2, 2 * ny : 6 * ny] = own_ref[p * inner : (p + 1) * inner]
        e_ref[p + 4, 2 * ny : 6 * ny] = xh_ref[p * inner : (p + 1) * inner]
    for p in range(6):
        e_ref[p, 0 : 2 * ny] = zl_ref[p * 2 * ny : (p + 1) * 2 * ny]
        e_ref[p, 6 * ny : 8 * ny] = zh_ref[p * 2 * ny : (p + 1) * 2 * ny]
    x = e_ref[...].reshape(6 * plane, D).astype(F32)
    r = lax.rsqrt(jnp.mean(x * x, axis=-1, keepdims=True) + EPSILON)
    normed = (x * r).astype(BF16)
    ones = (iota((D, 1), 0) // HEAD_DIM == iota((1, D), 1) // HEAD_DIM).astype(F32).astype(BF16)

    k = mm(normed, wqkv_ref[D : 2 * D], NT)
    v = mm(normed, wqkv_ref[2 * D : 3 * D], NT)
    q = mm(normed[plane : 5 * plane], wqkv_ref[0:D], NT)
    scale = scale_ref[...]
    rk = lax.rsqrt(head_sums(k * k, ones) * (1.0 / HEAD_DIM) + EPSILON)
    rq = lax.rsqrt(head_sums(q * q, ones) * (1.0 / HEAD_DIM) + EPSILON)
    kb = (k * rk).astype(BF16)
    vb = v.astype(BF16)
    qf = q * rq * scale

    def cot_source(i):
        px = i // qplane
        rest = i - px * qplane
        pz = rest // ny
        py = rest - pz * ny
        src = py // yb
        return ((src * 4 + px) * yb + (py - src * yb)) * 6 + pz

    cot = mm(select_rows(4 * qplane, cot_source), cot_ref[...])
    upf = mm(cot.astype(BF16), wout_ref[...])

    gx_pos = pos_ref[0]
    gy_pos = pos_ref[1]
    qi = iota((2 * qplane, 1), 0)
    qx = jnp.where(qi >= qplane, 1, 0)
    qr = qi - qx * qplane
    qz = qr // ny
    qy = qr - qz * ny
    kj = iota((1, 4 * plane), 1)
    kx = kj // plane
    kr = kj - kx * plane
    kz = kr // ny
    ky = kr - kz * ny
    dx = kx - qx
    dz = kz - qz
    dy = ky - qy
    near = (dx >= 0) & (dx <= 2) & (dz >= 0) & (dz <= 2) & (dy >= -1) & (dy <= 1)
    gz = gy_pos * 4 - 2 + kz
    z_ok = (gz >= 0) & (gz < total_z)

    for b in range(2):
        gxk = gx_pos * 2 - 2 + 2 * b + kx
        ok = near & (z_ok & (gxk >= 0) & (gxk < total_x))
        bias = jnp.where(ok, 0.0, NEGATIVE)
        q0 = 2 * b * plane + ny
        qblk = jnp.concatenate(
            [qf[q0 : q0 + qplane], qf[q0 + plane : q0 + plane + qplane]], axis=0
        ).astype(BF16)
        kblk = kb[2 * b * plane : (2 * b + 4) * plane]
        vblk = vb[2 * b * plane : (2 * b + 4) * plane]
        ublk = upf[2 * b * qplane : (2 * b + 2) * qplane].astype(BF16)
        own0 = (qplane if b == 0 else 0) + ny
        col0 = 2 * plane if b == 0 else 0
        for h in range(HEADS):
            lanes = slice(h * HEAD_DIM, (h + 1) * HEAD_DIM)
            qh, kh, vh, uh = qblk[:, lanes], kblk[:, lanes], vblk[:, lanes], ublk[:, lanes]
            s = mm(qh, kh, NT) + bias
            w = jnp.exp(s - jnp.max(s, axis=-1, keepdims=True))
            w = w * (1.0 / jnp.sum(w, axis=-1, keepdims=True))
            dp = mm(uh, vh, NT)
            ds = w * (dp - jnp.sum(w * dp, axis=-1, keepdims=True))
            att_ref[b * inner : (b + 1) * inner, lanes] = mm(
                w[own0 : own0 + inner].astype(BF16), vh
            )
            dq_ref[b * inner : (b + 1) * inner, lanes] = mm(
                ds[own0 : own0 + inner].astype(BF16), kh
            )
            dk = mm(ds[:, col0 : col0 + 2 * plane].astype(BF16), qh, TN)
            dv = mm(w[:, col0 : col0 + 2 * plane].astype(BF16), uh, TN)
            if b == 0:
                dk_ref[:, lanes] = dk
                dv_ref[:, lanes] = dv
            else:
                dk_ref[:, lanes] += dk
                dv_ref[:, lanes] += dv

    def own_rows(values, planes, start, first):
        return jnp.concatenate(
            [values[(first + p) * planes + start : (first + p) * planes + start + inner] for p in range(2)],
            axis=0,
        )

    q_o = own_rows(q, plane, 2 * ny, 1)
    rq_o = own_rows(rq, plane, 2 * ny, 1)
    k_o = own_rows(k, plane, 2 * ny, 2)
    rk_o = own_rows(rk, plane, 2 * ny, 2)
    x_o = own_rows(x, plane, 2 * ny, 2)
    r_o = own_rows(r, plane, 2 * ny, 2)
    cot_o = own_rows(cot, qplane, ny, 1)
    dk_o = own_rows(dk_ref[...], plane, 2 * ny, 0)
    dv_o = own_rows(dv_ref[...], plane, 2 * ny, 0)
    gq = dq_ref[...] * scale
    inv = 1.0 / HEAD_DIM
    gq_b = (rq_o * gq - q_o * (rq_o * rq_o * rq_o) * (head_sums(q_o * gq, ones) * inv)).astype(BF16)
    gk_b = (rk_o * dk_o - k_o * (rk_o * rk_o * rk_o) * (head_sums(k_o * dk_o, ones) * inv)).astype(BF16)
    gv_b = dv_o.astype(BF16)
    att_b = att_ref[...].astype(BF16)
    cot_b = cot_o.astype(BF16)
    normed_b = (x_o * r_o).astype(BF16)

    width = 4 * D // n_gx
    per = D // width
    for d in range(n_gx):
        part = (gq_b, gk_b, gv_b, cot_b)[d // per]
        off = (d % per) * width
        send_ref[d, :, 0:width] = part[:, off : off + width]
        send_ref[d, :, width : width + D] = normed_b if d < 3 * per else att_b

    g_norm = mm(gq_b, wqkv_ref[0:D]) + mm(gk_b, wqkv_ref[D : 2 * D]) + mm(gv_b, wqkv_ref[2 * D : 3 * D])
    g_in = r_o * g_norm - x_o * (r_o * r_o * r_o) * jnp.mean(x_o * g_norm, axis=-1, keepdims=True)
    gin = (cot_o + g_in).astype(BF16)

    def gin_source(i):
        px = i // inner
        rest = i - px * inner
        py = rest // 4
        return px * inner + (rest - py * 4) * ny + py

    gin_ref[...] = mm(select_rows(tokens, gin_source), gin).astype(BF16)

    out = (x_o + mm(att_b, wout_ref[...], NT)).astype(BF16)

    def out_source(i):
        dst = i // (2 * yb * 4)
        rest = i - dst * (2 * yb * 4)
        px = rest // (yb * 4)
        rest = rest - px * (yb * 4)
        py = rest // 4
        return px * inner + (rest - py * 4) * ny + dst * yb + py

    out_ref[...] = mm(select_rows(tokens, out_source), out).astype(BF16)


def partial_kernel(recv_ref, out_ref, send_ref, *, width, n_gy, extra):
    n_gx, tokens, _ = recv_ref.shape
    both = recv_ref[...].reshape(n_gx * tokens, width + D)
    partial = mm(both[:, 0:width], both[:, width : width + D], TN).astype(BF16)
    rows = width // n_gy
    for d in range(n_gy):
        send_ref[d, 0:rows] = partial[d * rows : (d + 1) * rows]
        send_ref[d, rows : rows + extra] = out_ref[d * extra : (d + 1) * extra]


def final_kernel(recv_ref, gw_ref, out_ref, *, rows, extra, factor):
    n_gy = recv_ref.shape[0]
    total = recv_ref[0, 0:rows].astype(F32)
    for s in range(1, n_gy):
        total = total + recv_ref[s, 0:rows].astype(F32)
    gw_ref[...] = total * factor
    got = jnp.concatenate([recv_ref[s, rows : rows + extra].astype(F32) for s in range(n_gy)], axis=0)

    def source(i):
        xy = i // (4 * n_gy)
        rest = i - xy * (4 * n_gy)
        src = rest // 4
        return src * extra + xy * 4 + rest - src * 4

    out_ref[...] = mm(select_rows(n_gy * extra, source), got.astype(BF16)).astype(BF16)


def on_device(slab_tokens, cotangent, w_qkv, w_out, logit_scale):
    size_x, ny, size_z, _ = slab_tokens.shape
    n_gx = lax.axis_size("gx")
    n_gy = lax.axis_size("gy")
    yb = cotangent.shape[1]
    total_x, total_z = size_x * n_gx, size_z * n_gy
    assert size_x == 2 and size_z == 4 and cotangent.shape[0] == 2
    assert cotangent.shape[2] == total_z and yb * n_gy == ny
    tokens = size_x * ny * size_z
    up_x = [(i, i + 1) for i in range(n_gx - 1)]
    down_x = [(t, s) for s, t in up_x]
    up_y = [(i, i + 1) for i in range(n_gy - 1)]
    down_y = [(t, s) for s, t in up_y]

    own = jnp.transpose(slab_tokens, (0, 2, 1, 3))
    own_rows = own.reshape(tokens, D)
    from_low = lax.ppermute(
        jnp.concatenate([own_rows, cotangent[1].reshape(-1, D)], axis=0), "gx", up_x
    )
    from_high = lax.ppermute(
        jnp.concatenate([own_rows, cotangent[0].reshape(-1, D)], axis=0), "gx", down_x
    )
    low_slab = from_low[:tokens].reshape(2, 4, ny, D)
    high_slab = from_high[:tokens].reshape(2, 4, ny, D)

    def z_edge(start):
        return jnp.concatenate(
            [a[:, start : start + 2] for a in (low_slab, own, high_slab)], axis=0
        ).reshape(-1, D)

    z_low = lax.ppermute(z_edge(2), "gy", up_y)
    z_high = lax.ppermute(z_edge(0), "gy", down_y)
    cot4 = jnp.concatenate(
        [
            from_low[tokens:].reshape(1, yb, total_z, D),
            cotangent,
            from_high[tokens:].reshape(1, yb, total_z, D),
        ],
        axis=0,
    )
    padded = jnp.pad(cot4, ((0, 0), (0, 0), (1, 1), (0, 0)))
    windows = jnp.stack([padded[:, :, 4 * d : 4 * d + 6] for d in range(n_gy)])
    cot_rows = lax.all_to_all(windows, "gy", 0, 0, tiled=True).reshape(-1, D)

    scale = jnp.repeat(logit_scale / HEAD_DIM, HEAD_DIM)[None]
    pos = jnp.stack([lax.axis_index("gx"), lax.axis_index("gy")]).astype(jnp.int32)
    width = 4 * D // n_gx
    vmem = pl.BlockSpec(memory_space=pltpu.VMEM)
    send, out_rows, gin = pl.pallas_call(
        lambda *refs: main_kernel(
            *refs, ny=ny, n_gx=n_gx, n_gy=n_gy, total_x=total_x, total_z=total_z
        ),
        name="layer",
        out_shape=(
            jax.ShapeDtypeStruct((n_gx, tokens, width + D), BF16),
            jax.ShapeDtypeStruct((tokens, D), BF16),
            jax.ShapeDtypeStruct((tokens, D), BF16),
        ),
        in_specs=[pl.BlockSpec(memory_space=pltpu.SMEM)] + [vmem] * 9,
        out_specs=(vmem, vmem, vmem),
        scratch_shapes=[
            pltpu.VMEM((6, 8 * ny, D), BF16),
            pltpu.VMEM((tokens, D), F32),
            pltpu.VMEM((16 * ny, D), F32),
            pltpu.VMEM((16 * ny, D), F32),
            pltpu.VMEM((tokens, D), F32),
        ],
    )(pos, own_rows, from_low, from_high, z_low, z_high, cot_rows, w_qkv, w_out, scale)

    recv = lax.all_to_all(send, "gx", 0, 0, tiled=True)
    extra = tokens // n_gy
    rows = width // n_gy
    send2 = pl.pallas_call(
        lambda *refs: partial_kernel(*refs, width=width, n_gy=n_gy, extra=extra),
        name="partial",
        out_shape=jax.ShapeDtypeStruct((n_gy, rows + extra, D), BF16),
        in_specs=[vmem, vmem],
        out_specs=vmem,
    )(recv, out_rows)
    recv2 = lax.all_to_all(send2, "gy", 0, 0, tiled=True)
    factor = 1.0 / math.sqrt(total_x * ny * total_z)
    grad_weights, output = pl.pallas_call(
        lambda *refs: final_kernel(*refs, rows=rows, extra=extra, factor=factor),
        name="final",
        out_shape=(
            jax.ShapeDtypeStruct((rows, D), F32),
            jax.ShapeDtypeStruct((n_gy * extra, D), BF16),
        ),
        in_specs=[vmem],
        out_specs=(vmem, vmem),
    )(recv2)
    return (
        output.reshape(2, yb, total_z, D),
        gin.reshape(2, ny, 4, D),
        grad_weights,
    )


def solution(mesh):
    return jax.shard_map(
        on_device,
        mesh=mesh,
        in_specs=(P("gx", None, "gy", None), P("gx", "gy", None, None), P(), P(), P()),
        out_specs=(P("gx", "gy", None, None), P("gx", None, "gy", None), P(("gx", "gy"), None)),
        check_vma=False,
    )
```

```python
import math

import jax
import jax.numpy as jnp
from jax import lax
from jax.experimental import pallas as pl
from jax.experimental.pallas import tpu as pltpu
from jax.sharding import PartitionSpec as P

D = 512
HEADS = 8
HEAD_DIM = 64
QUAD = 4
LANES = QUAD * HEAD_DIM
EPSILON = 1e-06
NEGATIVE = -1e30
F32 = jnp.float32
BF16 = jnp.bfloat16

NN = (((1,), (0,)), ((), ()))
NT = (((1,), (1,)), ((), ()))
TN = (((0,), (0,)), ((), ()))


def mm(a, b, dims=NN):
    return lax.dot_general(a, b, dims, preferred_element_type=F32)


def iota(shape, dim):
    return lax.broadcasted_iota(jnp.int32, shape, dim)


def head_sums(values, ones):
    high = values.astype(BF16)
    low = (values - high.astype(F32)).astype(BF16)
    return jnp.concatenate(
        [
            mm(high[:, g : g + LANES], ones) + mm(low[:, g : g + LANES], ones)
            for g in range(0, D, LANES)
        ],
        axis=1,
    )


def one_hot_rows(count, columns, source_of):
    return jnp.where(source_of(iota((count, 1), 0)) == iota((1, columns), 1), 1.0, 0.0).astype(BF16)


def pack_x_kernel(own_ref, cot_ref, m1_ref, m2_ref):
    tokens = own_ref.shape[0]
    odd = lax.axis_index("gx") % 2
    own = own_ref[...]
    m1_ref[0:tokens] = own
    m2_ref[0:tokens] = own
    m1_ref[tokens:] = cot_ref[1 - odd]
    m2_ref[tokens:] = cot_ref[odd]


def pack_z_kernel(own_ref, m1_ref, m2_ref, cot_ref, z1_ref, z2_ref, win_ref, *, ny, n_gx, n_gy):
    inner = 4 * ny
    tokens = 2 * inner
    edge = 2 * ny
    yb = ny // n_gy
    total_z = 4 * n_gy
    gx = lax.axis_index("gx")
    odd = gx % 2
    odd_z = lax.axis_index("gy") % 2
    for ref, off in ((z1_ref, (1 - odd_z) * edge), (z2_ref, odd_z * edge)):
        for i, src in enumerate((m1_ref, own_ref, m2_ref)):
            for p in range(2):
                start = pl.multiple_of(p * inner + off, edge)
                ref[(2 * i + p) * edge : (2 * i + p + 1) * edge] = src[pl.ds(start, edge)]
    planes = jnp.concatenate([m1_ref[tokens:], cot_ref[0], cot_ref[1], m2_ref[tokens:]], axis=0)

    def source(i):
        dst = i // (24 * yb)
        rest = i - dst * (24 * yb)
        px = rest // (6 * yb)
        rest = rest - px * (6 * yb)
        pz = rest // yb
        y = rest - pz * yb
        z = 4 * dst - 1 + pz
        outer = jnp.where(px == 0, jnp.where(odd == 0, 3, 0), jnp.where(odd == 0, 0, 3))
        slot = jnp.where((px == 0) | (px == 3), outer, px)
        x = gx * 2 - 1 + px
        ok = (z >= 0) & (z < total_z) & (x >= 0) & (x < 2 * n_gx)
        return jnp.where(ok, (slot * yb + y) * total_z + z, -1)

    rows = n_gy * 24 * yb
    win = mm(one_hot_rows(rows, 4 * yb * total_z, source), planes).astype(BF16)
    for d in range(n_gy):
        win_ref[d] = win[d * 24 * yb : (d + 1) * 24 * yb]


def main_kernel(
    ls_ref, own_ref, m1_ref, m2_ref, z1_ref, z2_ref, cot_ref, wqkv_ref, wout_ref,
    send_ref, out_ref, gin_ref,
    e_ref, bias_ref, dq_ref, dk_ref, dv_ref, att_ref,
    *, ny, n_gx, n_gy,
):
    plane = 8 * ny
    inner = 4 * ny
    edge = 2 * ny
    block = 12 * ny
    tokens = 2 * inner
    yb = ny // n_gy
    total_x, total_z = 2 * n_gx, 4 * n_gy
    gx = lax.axis_index("gx")
    gy = lax.axis_index("gy")
    odd = gx % 2
    odd_z = gy % 2
    base1 = 4 - 4 * odd
    base2 = 4 * odd
    for i, (src, base) in enumerate(((m1_ref, base1), (own_ref, 2), (m2_ref, base2))):
        for p in range(2):
            e_ref[base + p, edge : edge + inner] = src[p * inner : (p + 1) * inner]
            for ref, at in ((z1_ref, (1 - odd_z) * 6 * ny), (z2_ref, odd_z * 6 * ny)):
                at = pl.multiple_of(at, edge)
                e_ref[base + p, pl.ds(at, edge)] = ref[(2 * i + p) * edge : (2 * i + p + 1) * edge]

    x = e_ref[...].reshape(6 * plane, D).astype(F32)
    r = lax.rsqrt(jnp.mean(x * x, axis=-1, keepdims=True) + EPSILON)
    normed_f = x * r
    normed = normed_f.astype(BF16)

    def query_rows(values):
        parts = []
        for own_plane, other in ((2, 1), (3, 4)):
            a, o = own_plane * plane, other * plane
            parts += [
                values[a + 2 * ny : a + 6 * ny],
                values[a + ny : a + 2 * ny],
                values[a + 6 * ny : a + 7 * ny],
                values[o + ny : o + 7 * ny],
            ]
        return jnp.concatenate(parts, axis=0)

    def cot_source(i):
        b = i // block
        t = i - b * block
        own_x = 1 + b
        other_x = 3 * b
        t4 = t - 6 * ny
        zo = t4 // ny
        z_own = jnp.where(t < 4 * ny, 1 + t // ny, jnp.where(t < 5 * ny, 0, 5))
        is_own = t < 6 * ny
        px = jnp.where(is_own, own_x, other_x)
        pz = jnp.where(is_own, z_own, zo)
        y = t % ny
        src = y // yb
        return ((src * 4 + px) * 6 + pz) * yb + (y - src * yb)

    ones = (iota((LANES, 1), 0) // HEAD_DIM == iota((1, LANES), 1) // HEAD_DIM)
    ones = jnp.where(ones, 1.0, 0.0).astype(BF16)
    head = iota((1, D), 1) // HEAD_DIM
    scale = jnp.zeros((1, D), F32)
    for h in range(HEADS):
        scale = jnp.where(head == h, ls_ref[h] * (1.0 / HEAD_DIM), scale)

    k = mm(normed, wqkv_ref[D : 2 * D], NT)
    v = mm(normed, wqkv_ref[2 * D : 3 * D], NT)
    q = mm(query_rows(normed_f).astype(BF16), wqkv_ref[0:D], NT)
    rk = lax.rsqrt(head_sums(k * k, ones) * (1.0 / HEAD_DIM) + EPSILON)
    rq = lax.rsqrt(head_sums(q * q, ones) * (1.0 / HEAD_DIM) + EPSILON)
    kb = (k * rk).astype(BF16)
    vb = v.astype(BF16)
    qb = (q * rq * scale).astype(BF16)
    cot = mm(one_hot_rows(2 * block, 2 * block, cot_source), cot_ref[...])
    ub = mm(cot.astype(BF16), wout_ref[...]).astype(BF16)

    lane = iota((1, QUAD * block), 1)
    is_own = lane < QUAD * inner
    t_own = lane % inner
    t_oth = (lane - QUAD * inner) % (8 * ny)
    in_edge = t_oth < 2 * ny
    qz = jnp.where(
        is_own,
        2 + t_own // ny,
        jnp.where(in_edge, jnp.where(t_oth < ny, 1, 6), 1 + (t_oth - 2 * ny) // ny),
    )
    qy = lane % ny
    own_plane = is_own | in_edge
    kj = iota((4 * plane, 1), 0)
    kx = kj // plane
    kr = kj - kx * plane
    kz = kr // ny
    ky = kr - kz * ny
    gz = gy * 4 - 2 + kz
    z_ok = (gz >= 0) & (gz < total_z)
    near_zy = (jnp.abs(kz - qz) <= 1) & (jnp.abs(ky - qy) <= 1)

    mask = [
        jnp.where(iota((1, LANES), 1) // HEAD_DIM == j, 1.0, 0.0).astype(BF16) for j in range(QUAD)
    ]
    for b in range(2):
        qx = jnp.where(own_plane, 2 - b, 1 + b)
        gxk = gx * 2 - 2 + 2 * b + kx
        k_ok = z_ok & (gxk >= 0) & (gxk < total_x)
        ok = near_zy & (jnp.abs(kx - qx) <= 1) & k_ok
        bias_ref[...] = jnp.where(ok, 0.0, NEGATIVE)
        first = 2 * plane if b == 0 else 0
        for g in range(0, D, LANES):
            lanes = slice(g, g + LANES)
            kq = kb[2 * b * plane : (2 * b + 4) * plane, lanes]
            vq = vb[2 * b * plane : (2 * b + 4) * plane, lanes]

            def stacked(values):
                own_part = values[b * block : b * block + inner, lanes]
                other = values[b * block + inner : (b + 1) * block, lanes]
                return jnp.concatenate(
                    [own_part * m for m in mask] + [other * m for m in mask], axis=0
                )

            qs = stacked(qb)
            us = stacked(ub)
            s = mm(kq, qs, NT) + bias_ref[...]
            w = jnp.exp(s - jnp.max(s, axis=0, keepdims=True))
            w = w * (1.0 / jnp.sum(w, axis=0, keepdims=True))
            dp = mm(vq, us, NT)
            ds = w * (dp - jnp.sum(w * dp, axis=0, keepdims=True))
            wb = w.astype(BF16)
            dsb = ds.astype(BF16)
            o_all = mm(wb[:, 0 : QUAD * inner], vq, TN)
            dq_all = mm(dsb[:, 0 : QUAD * inner], kq, TN)
            lane_head = iota((1, LANES), 1) // HEAD_DIM
            att = o_all[0:inner]
            dq = dq_all[0:inner]
            for j in range(1, QUAD):
                att = jnp.where(lane_head == j, o_all[j * inner : (j + 1) * inner], att)
                dq = jnp.where(lane_head == j, dq_all[j * inner : (j + 1) * inner], dq)
            att_ref[b * inner : (b + 1) * inner, lanes] = att
            dq_ref[b * inner : (b + 1) * inner, lanes] = dq

            def own_keys(values):
                return jnp.concatenate(
                    [values[first + p * plane + edge : first + p * plane + edge + inner] for p in range(2)],
                    axis=0,
                )

            dk = mm(own_keys(dsb), qs)
            dv = mm(own_keys(wb), us)
            if b == 0:
                dk_ref[:, lanes] = dk
                dv_ref[:, lanes] = dv
            else:
                dk_ref[:, lanes] += dk
                dv_ref[:, lanes] += dv

    def own_queries(values):
        return jnp.concatenate([values[0:inner], values[block : block + inner]], axis=0)

    def own_rows(values):
        return jnp.concatenate(
            [values[(2 + p) * plane + edge : (2 + p) * plane + edge + inner] for p in range(2)],
            axis=0,
        )

    q_o, rq_o, cot_o = own_queries(q), own_queries(rq), own_queries(cot)
    k_o, rk_o, x_o, r_o = own_rows(k), own_rows(rk), own_rows(x), own_rows(r)
    dk_o = dk_ref[...]
    gq = dq_ref[...] * scale
    inv = 1.0 / HEAD_DIM
    gq_b = (rq_o * gq - q_o * (rq_o * rq_o * rq_o) * (head_sums(q_o * gq, ones) * inv)).astype(BF16)
    gk_b = (rk_o * dk_o - k_o * (rk_o * rk_o * rk_o) * (head_sums(k_o * dk_o, ones) * inv)).astype(BF16)
    gv_b = dv_ref[...].astype(BF16)
    att_b = att_ref[...].astype(BF16)
    cot_b = cot_o.astype(BF16)
    normed_b = (x_o * r_o).astype(BF16)

    width = 4 * D // n_gx
    per = D // width
    for d in range(n_gx):
        part = (gq_b, gk_b, gv_b, cot_b)[d // per]
        off = (d % per) * width
        send_ref[d, :, 0:width] = part[:, off : off + width]
        send_ref[d, :, width : width + D] = normed_b if d < 3 * per else att_b

    g_norm = mm(gq_b, wqkv_ref[0:D]) + mm(gk_b, wqkv_ref[D : 2 * D]) + mm(gv_b, wqkv_ref[2 * D : 3 * D])
    g_in = r_o * g_norm - x_o * (r_o * r_o * r_o) * jnp.mean(x_o * g_norm, axis=-1, keepdims=True)
    gin = (cot_o + g_in).astype(BF16)

    def gin_source(i):
        px = i // inner
        rest = i - px * inner
        py = rest // 4
        return px * inner + (rest - py * 4) * ny + py

    gin_ref[...] = mm(one_hot_rows(tokens, tokens, gin_source), gin).astype(BF16)

    out = (x_o + mm(att_b, wout_ref[...], NT)).astype(BF16)

    def out_source(i):
        dst = i // (8 * yb)
        rest = i - dst * (8 * yb)
        px = rest // (4 * yb)
        rest = rest - px * (4 * yb)
        py = rest // 4
        return px * inner + (rest - py * 4) * ny + dst * yb + py

    out_ref[...] = mm(one_hot_rows(tokens, tokens, out_source), out).astype(BF16)


def partial_kernel(recv_ref, out_ref, send_ref, *, width, n_gy, extra):
    n_gx, tokens, _ = recv_ref.shape
    both = recv_ref[...].reshape(n_gx * tokens, width + D)
    partial = mm(both[:, 0:width], both[:, width : width + D], TN).astype(BF16)
    rows = width // n_gy
    for d in range(n_gy):
        send_ref[d, 0:rows] = partial[d * rows : (d + 1) * rows]
        send_ref[d, rows : rows + extra] = out_ref[d * extra : (d + 1) * extra]


def final_kernel(recv_ref, gw_ref, out_ref, *, rows, extra, factor):
    n_gy = recv_ref.shape[0]
    total = recv_ref[0, 0:rows].astype(F32)
    for s in range(1, n_gy):
        total = total + recv_ref[s, 0:rows].astype(F32)
    gw_ref[...] = total * factor
    got = jnp.concatenate([recv_ref[s, rows : rows + extra] for s in range(n_gy)], axis=0)

    def source(i):
        xy = i // (4 * n_gy)
        rest = i - xy * (4 * n_gy)
        src = rest // 4
        return src * extra + xy * 4 + rest - src * 4

    out_ref[...] = mm(one_hot_rows(n_gy * extra, n_gy * extra, source), got).astype(BF16)


def matchings(count, wrap):
    first = [(i, i ^ 1) for i in range(count)]
    ends = [(0, count - 1), (count - 1, 0)] if wrap else [(0, 0), (count - 1, count - 1)]
    second = ends + [(i, i + 1) for i in range(1, count - 1, 2)]
    second += [(i + 1, i) for i in range(1, count - 1, 2)]
    return first, second


def call(kernel, name, args, outs, scratch=(), smem=0):
    vmem = pl.BlockSpec(memory_space=pltpu.VMEM)
    args = list(args[:smem]) + [
        pltpu.with_memory_space_constraint(a, pltpu.VMEM) for a in args[smem:]
    ]
    return pl.pallas_call(
        kernel,
        name=name,
        out_shape=tuple(jax.ShapeDtypeStruct(s, t) for s, t in outs),
        in_specs=[pl.BlockSpec(memory_space=pltpu.SMEM)] * smem + [vmem] * (len(args) - smem),
        out_specs=(vmem,) * len(outs),
        scratch_shapes=[pltpu.VMEM(s, t) for s, t in scratch],
    )(*args)


def on_device(slab_tokens, cotangent, w_qkv, w_out, logit_scale):
    size_x, ny, size_z, _ = slab_tokens.shape
    n_gx = lax.axis_size("gx")
    n_gy = lax.axis_size("gy")
    yb = cotangent.shape[1]
    total_x, total_z = size_x * n_gx, size_z * n_gy
    assert size_x == 2 and size_z == 4 and cotangent.shape[0] == 2
    assert cotangent.shape[2] == total_z and yb * n_gy == ny
    tokens = size_x * ny * size_z
    gx1, gx2 = matchings(n_gx, True)
    gy1, gy2 = matchings(n_gy, False)

    own = jnp.transpose(slab_tokens, (0, 2, 1, 3)).reshape(tokens, D)
    cot = cotangent.reshape(2, yb * total_z, D)
    x_payload = ((tokens + yb * total_z, D), BF16)
    p1, p2 = call(pack_x_kernel, "pack_x", (own, cot), (x_payload, x_payload))
    m1 = lax.ppermute(p1, "gx", gx1)
    m2 = lax.ppermute(p2, "gx", gx2)

    z_payload = ((12 * ny, D), BF16)
    s1, s2, windows = call(
        lambda *refs: pack_z_kernel(*refs, ny=ny, n_gx=n_gx, n_gy=n_gy),
        "pack_z",
        (own, m1, m2, cot),
        (z_payload, z_payload, ((n_gy, 24 * yb, D), BF16)),
    )
    z1 = lax.ppermute(s1, "gy", gy1)
    z2 = lax.ppermute(s2, "gy", gy2)
    cot_rows = lax.all_to_all(windows, "gy", 0, 0, tiled=True).reshape(24 * ny, D)

    width = 4 * D // n_gx
    send, out_rows, gin = call(
        lambda *refs: main_kernel(*refs, ny=ny, n_gx=n_gx, n_gy=n_gy),
        "layer",
        (logit_scale, own, m1, m2, z1, z2, cot_rows, w_qkv, w_out),
        (((n_gx, tokens, width + D), BF16), ((tokens, D), BF16), ((tokens, D), BF16)),
        scratch=(
            ((6, 8 * ny, D), BF16),
            ((32 * ny, QUAD * 12 * ny), F32),
            ((tokens, D), F32),
            ((tokens, D), F32),
            ((tokens, D), F32),
            ((tokens, D), F32),
        ),
        smem=1,
    )

    recv = lax.all_to_all(send, "gx", 0, 0, tiled=True)
    extra = tokens // n_gy
    rows = width // n_gy
    (send2,) = call(
        lambda *refs: partial_kernel(*refs, width=width, n_gy=n_gy, extra=extra),
        "partial",
        (recv, out_rows),
        (((n_gy, rows + extra, D), BF16),),
    )
    recv2 = lax.all_to_all(send2, "gy", 0, 0, tiled=True)
    factor = 1.0 / math.sqrt(total_x * ny * total_z)
    grad_weights, output = call(
        lambda *refs: final_kernel(*refs, rows=rows, extra=extra, factor=factor),
        "final",
        (recv2,),
        (((rows, D), F32), ((n_gy * extra, D), BF16)),
    )
    return (
        output.reshape(2, yb, total_z, D),
        gin.reshape(2, ny, 4, D),
        grad_weights,
    )


def solution(mesh):
    return jax.shard_map(
        on_device,
        mesh=mesh,
        in_specs=(P("gx", None, "gy", None), P("gx", "gy", None, None), P(), P(), P()),
        out_specs=(P("gx", "gy", None, None), P("gx", None, "gy", None), P(("gx", "gy"), None)),
        check_vma=False,
    )
```

```python
import math

import jax
import jax.numpy as jnp
from jax import lax
from jax.experimental import pallas as pl
from jax.experimental.pallas import tpu as pltpu
from jax.sharding import PartitionSpec as P

D = 512
HEADS = 8
HEAD_DIM = 64
QUAD = 4
LANES = QUAD * HEAD_DIM
EPSILON = 1e-06
NEGATIVE = -1e30
F32 = jnp.float32
BF16 = jnp.bfloat16

NN = (((1,), (0,)), ((), ()))
NT = (((1,), (1,)), ((), ()))
TN = (((0,), (0,)), ((), ()))


def mm(a, b, dims=NN):
    return lax.dot_general(a, b, dims, preferred_element_type=F32)


def iota(shape, dim):
    return lax.broadcasted_iota(jnp.int32, shape, dim)


def head_sums(values, ones):
    high = values.astype(BF16)
    low = (values - high.astype(F32)).astype(BF16)
    return jnp.concatenate(
        [
            mm(high[:, g : g + LANES], ones) + mm(low[:, g : g + LANES], ones)
            for g in range(0, D, LANES)
        ],
        axis=1,
    )


def one_hot_rows(count, columns, source_of):
    return jnp.where(source_of(iota((count, 1), 0)) == iota((1, columns), 1), 1.0, 0.0).astype(BF16)


def pack_z_kernel(own_ref, cot_ref, *outs, ny, n_gy):
    inner = 4 * ny
    edge = 2 * ny
    yb = ny // n_gy
    total_z = 4 * n_gy
    window = 12 * yb
    gy = lax.axis_index("gy")
    odd = gy % 2

    def source(i):
        k = i // window
        rest = i - k * window
        px = rest // (6 * yb)
        rest = rest - px * (6 * yb)
        pz = rest // yb
        z = 4 * (gy ^ k) - 1 + pz
        return jnp.where((z >= 0) & (z < total_z), (px * yb + rest - pz * yb) * total_z + z, -1)

    win = mm(one_hot_rows(n_gy * window, 2 * yb * total_z, source), cot_ref[...]).astype(BF16)
    for k in range(n_gy):
        outs[k][0:window] = win[k * window : (k + 1) * window]
    last = 3 if n_gy == 4 else n_gy
    base = window if n_gy == 4 else 0
    for ref, start, off in ((outs[1], window, 1 - odd), (outs[last], base, odd)):
        for p in range(2):
            at = pl.multiple_of(p * inner + off * edge, edge)
            ref[start + p * edge : start + (p + 1) * edge] = own_ref[pl.ds(at, edge)]


def pack_x_kernel(own_ref, *refs, ny, n_gy):
    ins, (w1_ref, w2_ref, m1_ref, m2_ref, ext_ref, cot_ref) = refs[:-6], refs[-6:]
    inner = 4 * ny
    plane = 8 * ny
    edge = 2 * ny
    qplane = 6 * ny
    yb = ny // n_gy
    window = 12 * yb
    gx = lax.axis_index("gx")
    gy = lax.axis_index("gy")
    odd = gx % 2
    odd_z = gy % 2
    last = 3 if n_gy == 4 else n_gy
    base = window if n_gy == 4 else 0
    for p in range(2):
        ext_ref[p * plane + edge : p * plane + edge + inner] = own_ref[p * inner : (p + 1) * inner]
        for ref, start, top in ((ins[1], window, 1 - odd_z), (ins[last], base, odd_z)):
            at = pl.multiple_of(p * plane + top * qplane, edge)
            ext_ref[pl.ds(at, edge)] = ref[start + p * edge : start + (p + 1) * edge]
    got = jnp.concatenate([ins[k][0:window].astype(F32) for k in range(n_gy)], axis=0).astype(BF16)

    def source(i):
        row = i // ny
        y = i - row * ny
        src = y // yb
        return ((src ^ gy) * 12 + row) * yb + y - src * yb

    cot = mm(one_hot_rows(2 * qplane, n_gy * window, source), got).astype(BF16)
    cot_ref[0] = cot[0:qplane]
    cot_ref[1] = cot[qplane : 2 * qplane]
    for ref, p in ((m1_ref, 1 - odd), (m2_ref, odd)):
        ref[0 : 2 * plane] = ext_ref[...]
        ref[2 * plane :] = cot_ref[p]


def main_kernel(*refs, ny, n_gx, n_gy):
    ls_ref, ext_ref, m1_ref, m2_ref, cot_ref, wqkv_ref, wout_ref = refs[:7]
    pairs = n_gx // 2
    send_refs = refs[7 : 7 + pairs]
    out_ref, gin_ref, e_ref, c_ref, full_ref, bias_ref, dq_ref, dk_ref, dv_ref, att_ref = refs[7 + pairs :]
    plane = 8 * ny
    inner = 4 * ny
    qplane = 6 * ny
    edge = 2 * ny
    block = 12 * ny
    tokens = 2 * inner
    yb = ny // n_gy
    total_x, total_z = 2 * n_gx, 4 * n_gy
    gx = lax.axis_index("gx")
    gy = lax.axis_index("gy")
    odd = gx % 2
    for src, base in ((m1_ref, 4 - 4 * odd), (ext_ref, 2), (m2_ref, 4 * odd)):
        for p in range(2):
            e_ref[base + p] = src[p * plane : (p + 1) * plane]
    inside = jnp.where((gx > 0) & (gx < n_gx - 1), 1.0, 0.0)
    c_ref[1] = cot_ref[0]
    c_ref[2] = cot_ref[1]
    c_ref[3 - 3 * odd] = m1_ref[2 * plane :]
    c_ref[3 * odd] = (m2_ref[2 * plane :].astype(F32) * inside).astype(BF16)

    x = e_ref[...].reshape(6 * plane, D).astype(F32)
    r = lax.rsqrt(jnp.mean(x * x, axis=-1, keepdims=True) + EPSILON)
    normed_f = x * r
    normed = normed_f.astype(BF16)

    def query_rows(values, rows, halo):
        parts = []
        for own_plane, other in ((2, 1), (3, 4)):
            a, o = own_plane * rows - halo[0], other * rows - halo[0]
            first = halo[1]
            parts += [
                values[a + first + ny : a + first + 5 * ny],
                values[a + first : a + first + ny],
                values[a + first + 5 * ny : a + first + 6 * ny],
                values[o + first : o + first + 6 * ny],
            ]
        return jnp.concatenate(parts, axis=0)

    ones = (iota((LANES, 1), 0) // HEAD_DIM == iota((1, LANES), 1) // HEAD_DIM)
    ones = jnp.where(ones, 1.0, 0.0).astype(BF16)
    head = iota((1, D), 1) // HEAD_DIM
    scale = jnp.zeros((1, D), F32)
    for h in range(HEADS):
        scale = jnp.where(head == h, ls_ref[h] * (1.0 / HEAD_DIM), scale)

    k = mm(normed, wqkv_ref[D : 2 * D], NT)
    v = mm(normed, wqkv_ref[2 * D : 3 * D], NT)
    q = mm(query_rows(normed_f, plane, (0, ny)).astype(BF16), wqkv_ref[0:D], NT)
    rk = lax.rsqrt(head_sums(k * k, ones) * (1.0 / HEAD_DIM) + EPSILON)
    rq = lax.rsqrt(head_sums(q * q, ones) * (1.0 / HEAD_DIM) + EPSILON)
    kb = (k * rk).astype(BF16)
    vb = v.astype(BF16)
    qb = (q * rq * scale).astype(BF16)
    up = mm(c_ref[...].reshape(4 * qplane, D), wout_ref[...])
    ub = query_rows(up, qplane, (qplane, 0)).astype(BF16)

    lane = iota((1, QUAD * block), 1)
    is_own = lane < QUAD * inner
    t_own = lane % inner
    t_oth = (lane - QUAD * inner) % (8 * ny)
    in_edge = t_oth < 2 * ny
    qz = jnp.where(
        is_own,
        2 + t_own // ny,
        jnp.where(in_edge, jnp.where(t_oth < ny, 1, 6), 1 + (t_oth - 2 * ny) // ny),
    )
    qy = lane % ny
    own_plane = is_own | in_edge
    kj = iota((4 * plane, 1), 0)
    kx = kj // plane
    kr = kj - kx * plane
    kz = kr // ny
    ky = kr - kz * ny
    gz = gy * 4 - 2 + kz
    z_ok = (gz >= 0) & (gz < total_z)
    near_zy = (jnp.abs(kz - qz) <= 1) & (jnp.abs(ky - qy) <= 1)

    mask = [
        jnp.where(iota((1, LANES), 1) // HEAD_DIM == j, 1.0, 0.0).astype(BF16) for j in range(QUAD)
    ]
    for b in range(2):
        qx = jnp.where(own_plane, 2 - b, 1 + b)
        gxk = gx * 2 - 2 + 2 * b + kx
        k_ok = z_ok & (gxk >= 0) & (gxk < total_x)
        ok = near_zy & (jnp.abs(kx - qx) <= 1) & k_ok
        bias_ref[...] = jnp.where(ok, 0.0, NEGATIVE)
        first = 2 * plane if b == 0 else 0
        for g in range(0, D, LANES):
            lanes = slice(g, g + LANES)
            kq = kb[2 * b * plane : (2 * b + 4) * plane, lanes]
            vq = vb[2 * b * plane : (2 * b + 4) * plane, lanes]

            def stacked(values):
                own_part = values[b * block : b * block + inner, lanes]
                other = values[b * block + inner : (b + 1) * block, lanes]
                return jnp.concatenate(
                    [own_part * m for m in mask] + [other * m for m in mask], axis=0
                )

            qs = stacked(qb)
            us = stacked(ub)
            s = mm(kq, qs, NT) + bias_ref[...]
            w = jnp.exp(s - jnp.max(s, axis=0, keepdims=True))
            w = w * (1.0 / jnp.sum(w, axis=0, keepdims=True))
            dp = mm(vq, us, NT)
            ds = w * (dp - jnp.sum(w * dp, axis=0, keepdims=True))
            wb = w.astype(BF16)
            dsb = ds.astype(BF16)
            o_all = mm(wb[:, 0 : QUAD * inner], vq, TN)
            dq_all = mm(dsb[:, 0 : QUAD * inner], kq, TN)
            lane_head = iota((1, LANES), 1) // HEAD_DIM
            att = o_all[0:inner]
            dq = dq_all[0:inner]
            for j in range(1, QUAD):
                att = jnp.where(lane_head == j, o_all[j * inner : (j + 1) * inner], att)
                dq = jnp.where(lane_head == j, dq_all[j * inner : (j + 1) * inner], dq)
            att_ref[b * inner : (b + 1) * inner, lanes] = att
            dq_ref[b * inner : (b + 1) * inner, lanes] = dq

            def own_keys(values):
                return jnp.concatenate(
                    [values[first + p * plane + edge : first + p * plane + edge + inner] for p in range(2)],
                    axis=0,
                )

            dk = mm(own_keys(dsb), qs)
            dv = mm(own_keys(wb), us)
            if b == 0:
                dk_ref[:, lanes] = dk
                dv_ref[:, lanes] = dv
            else:
                dk_ref[:, lanes] += dk
                dv_ref[:, lanes] += dv

    def own_queries(values):
        return jnp.concatenate([values[0:inner], values[block : block + inner]], axis=0)

    def own_rows(values):
        return jnp.concatenate(
            [values[(2 + p) * plane + edge : (2 + p) * plane + edge + inner] for p in range(2)],
            axis=0,
        )

    q_o, rq_o = own_queries(q), own_queries(rq)
    cot_o = jnp.concatenate([c_ref[1 + p].astype(F32)[ny : 5 * ny] for p in range(2)], axis=0)
    k_o, rk_o, x_o, r_o = own_rows(k), own_rows(rk), own_rows(x), own_rows(r)
    dk_o = dk_ref[...]
    gq = dq_ref[...] * scale
    inv = 1.0 / HEAD_DIM
    gq_b = (rq_o * gq - q_o * (rq_o * rq_o * rq_o) * (head_sums(q_o * gq, ones) * inv)).astype(BF16)
    gk_b = (rk_o * dk_o - k_o * (rk_o * rk_o * rk_o) * (head_sums(k_o * dk_o, ones) * inv)).astype(BF16)
    gv_b = dv_ref[...].astype(BF16)
    att_b = att_ref[...].astype(BF16)
    cot_b = cot_o.astype(BF16)
    normed_b = (x_o * r_o).astype(BF16)

    width = 8 * D // n_gx
    per = D // width
    for d in range(pairs):
        part = (gq_b, gk_b, gv_b, cot_b)[d // per]
        off = (d % per) * width
        full_ref[d, :, 0:width] = part[:, off : off + width]
        full_ref[d, :, width : width + D] = normed_b if d < 3 * per else att_b
    for k in range(pairs):
        send_refs[k][...] = full_ref[(gx // 2) ^ k]

    g_norm = mm(gq_b, wqkv_ref[0:D]) + mm(gk_b, wqkv_ref[D : 2 * D]) + mm(gv_b, wqkv_ref[2 * D : 3 * D])
    g_in = r_o * g_norm - x_o * (r_o * r_o * r_o) * jnp.mean(x_o * g_norm, axis=-1, keepdims=True)
    gin = (cot_o + g_in).astype(BF16)

    def gin_source(i):
        px = i // inner
        rest = i - px * inner
        py = rest // 4
        return px * inner + (rest - py * 4) * ny + py

    gin_ref[...] = mm(one_hot_rows(tokens, tokens, gin_source), gin).astype(BF16)

    out = (x_o + mm(att_b, wout_ref[...], NT)).astype(BF16)

    def out_source(i):
        dst = i // (8 * yb)
        rest = i - dst * (8 * yb)
        px = rest // (4 * yb)
        rest = rest - px * (4 * yb)
        py = rest // 4
        return px * inner + (rest - py * 4) * ny + dst * yb + py

    moved = mm(one_hot_rows(tokens, tokens, out_source), out).astype(BF16)
    for d in range(n_gy):
        out_ref[d] = moved[d * 8 * yb : (d + 1) * 8 * yb]


def partial_kernel(*refs):
    ins, (mine_ref, other_ref, both_ref) = refs[:-3], refs[-3:]
    width = mine_ref.shape[0]
    left = jnp.concatenate([ref[:, 0 : 2 * width] for ref in ins], axis=0)
    right = jnp.concatenate([ref[:, 2 * width :] for ref in ins], axis=0)
    partial = mm(left, right, TN)
    both_ref[0] = partial[0:width]
    both_ref[1] = partial[width:]
    odd = lax.axis_index("gx") % 2
    mine_ref[...] = both_ref[odd]
    other_ref[...] = both_ref[1 - odd].astype(BF16)


def scatter_kernel(mine_ref, other_ref, out_ref, keep_ref, *refs, n_gy):
    sends, sum_ref = refs[:-1], refs[-1]
    rows, extra = keep_ref.shape[0], out_ref.shape[1]
    total = mine_ref[...] + other_ref[...].astype(F32)
    for d in range(n_gy):
        sum_ref[d] = total[d * rows : (d + 1) * rows]
    gy = lax.axis_index("gy")
    keep_ref[...] = sum_ref[gy]
    for k in range(1, n_gy):
        sends[k - 1][0:rows] = sum_ref[gy ^ k].astype(BF16)
        sends[k - 1][rows : rows + extra] = out_ref[gy ^ k]


def final_kernel(keep_ref, own_ref, *refs, n_gy, factor):
    ins, (gw_ref, out_ref, got_ref) = refs[:-3], refs[-3:]
    rows, extra = keep_ref.shape[0], own_ref.shape[1]
    gy = lax.axis_index("gy")
    total = keep_ref[...]
    got_ref[gy] = own_ref[gy]
    for k in range(1, n_gy):
        total = total + ins[k - 1][0:rows].astype(F32)
        got_ref[gy ^ k] = ins[k - 1][rows : rows + extra]
    gw_ref[...] = total * factor

    def source(i):
        xy = i // (4 * n_gy)
        rest = i - xy * (4 * n_gy)
        src = rest // 4
        return src * extra + xy * 4 + rest - src * 4

    got = got_ref[...].reshape(n_gy * extra, D)
    out_ref[...] = mm(one_hot_rows(n_gy * extra, n_gy * extra, source), got).astype(BF16)


def matchings(count):
    first = [(i, i ^ 1) for i in range(count)]
    second = [((i - 1) % count, i) for i in range(0, count, 2)]
    second += [(t, s) for s, t in second]
    return first, second


def call(kernel, name, args, outs, scratch=(), smem=0):
    vmem = pl.BlockSpec(memory_space=pltpu.VMEM)
    args = list(args[:smem]) + [
        pltpu.with_memory_space_constraint(a, pltpu.VMEM) for a in args[smem:]
    ]
    return pl.pallas_call(
        kernel,
        name=name,
        out_shape=tuple(jax.ShapeDtypeStruct(s, t) for s, t in outs),
        in_specs=[pl.BlockSpec(memory_space=pltpu.SMEM)] * smem + [vmem] * (len(args) - smem),
        out_specs=(vmem,) * len(outs),
        scratch_shapes=[pltpu.VMEM(s, t) for s, t in scratch],
    )(*args)


def on_device(slab_tokens, cotangent, w_qkv, w_out, logit_scale):
    size_x, ny, size_z, _ = slab_tokens.shape
    n_gx = lax.axis_size("gx")
    n_gy = lax.axis_size("gy")
    yb = cotangent.shape[1]
    total_x, total_z = size_x * n_gx, size_z * n_gy
    assert size_x == 2 and size_z == 4 and cotangent.shape[0] == 2
    assert cotangent.shape[2] == total_z and yb * n_gy == ny
    tokens = size_x * ny * size_z
    gx1, gx2 = matchings(n_gx)
    gy1, gy2 = matchings(n_gy)

    def swapped(value, axis, k):
        count = lax.axis_size(axis)
        return lax.ppermute(value, axis, [(i, i ^ k) for i in range(count)])

    own = jnp.transpose(slab_tokens, (0, 2, 1, 3)).reshape(tokens, D)
    cot = cotangent.reshape(2 * yb * total_z, D)
    window, edges = 12 * yb, 4 * ny
    merged = n_gy == 4
    sizes = [window + (edges if k == 1 or (merged and k == 3) else 0) for k in range(n_gy)]
    if not merged:
        sizes.append(edges)
    packed = call(
        lambda *refs: pack_z_kernel(*refs, ny=ny, n_gy=n_gy),
        "pack_z",
        (own, cot),
        [((s, D), BF16) for s in sizes],
    )
    order = [1] + ([3, 2] if merged else list(range(2, n_gy)))
    moved = {0: packed[0]}
    for k in order:
        moved[k] = swapped(packed[k], "gy", k)
    if not merged:
        moved[n_gy] = lax.ppermute(packed[n_gy], "gy", gy2)
    x_payload = ((16 * ny + 6 * ny, D), BF16)
    p1, p2, ext, cot_own = call(
        lambda *refs: pack_x_kernel(*refs, ny=ny, n_gy=n_gy),
        "pack_x",
        (own,) + tuple(moved[k] for k in range(len(sizes))) + (w_qkv, w_out),
        (x_payload, x_payload, ((16 * ny, D), BF16), ((2, 6 * ny, D), BF16)),
    )
    m1 = lax.ppermute(p1, "gx", gx1)
    m2 = lax.ppermute(p2, "gx", gx2)

    width = 4 * D // n_gx
    pairs = n_gx // 2
    extra = tokens // n_gy
    rows = width // n_gy
    results = call(
        lambda *refs: main_kernel(*refs, ny=ny, n_gx=n_gx, n_gy=n_gy),
        "layer",
        (logit_scale, ext, m1, m2, cot_own, w_qkv, w_out),
        [((tokens, 2 * width + D), BF16)] * pairs
        + [((n_gy, extra, D), BF16), ((tokens, D), BF16)],
        scratch=(
            ((6, 8 * ny, D), BF16),
            ((4, 6 * ny, D), BF16),
            ((pairs, tokens, 2 * width + D), BF16),
            ((32 * ny, QUAD * 12 * ny), F32),
            ((tokens, D), F32),
            ((tokens, D), F32),
            ((tokens, D), F32),
            ((tokens, D), F32),
        ),
        smem=1,
    )
    sends, out_rows, gin = results[:pairs], results[pairs], results[pairs + 1]
    arrived = [sends[0]] + [swapped(sends[k], "gx", 2 * k) for k in range(1, pairs)]
    mine, other = call(
        partial_kernel,
        "partial",
        arrived,
        (((width, D), F32), ((width, D), BF16)),
        scratch=(((2, width, D), F32),),
    )
    other = swapped(other, "gx", 1)
    keep, *blocks = call(
        lambda *refs: scatter_kernel(*refs, n_gy=n_gy),
        "scatter",
        (mine, other, out_rows),
        [((rows, D), F32)] + [((rows + extra, D), BF16)] * (n_gy - 1),
        scratch=(((n_gy, rows, D), F32),),
    )
    blocks = [swapped(blocks[k - 1], "gy", k) for k in range(1, n_gy)]
    factor = 1.0 / math.sqrt(total_x * ny * total_z)
    grad_weights, output = call(
        lambda *refs: final_kernel(*refs, n_gy=n_gy, factor=factor),
        "final",
        [keep, out_rows] + blocks,
        (((rows, D), F32), ((n_gy * extra, D), BF16)),
        scratch=(((n_gy, extra, D), BF16),),
    )
    return (
        output.reshape(2, yb, total_z, D),
        gin.reshape(2, ny, 4, D),
        grad_weights,
    )


def solution(mesh):
    return jax.shard_map(
        on_device,
        mesh=mesh,
        in_specs=(P("gx", None, "gy", None), P("gx", "gy", None, None), P(), P(), P()),
        out_specs=(P("gx", "gy", None, None), P("gx", None, "gy", None), P(("gx", "gy"), None)),
        check_vma=False,
    )
```

```python
import math

import jax
import jax.numpy as jnp
from jax import lax
from jax.experimental import pallas as pl
from jax.experimental.pallas import tpu as pltpu
from jax.sharding import PartitionSpec as P

D = 512
HEADS = 8
HEAD_DIM = 64
QUAD = 4
LANES = QUAD * HEAD_DIM
EPSILON = 1e-06
NEGATIVE = -1e30
F32 = jnp.float32
BF16 = jnp.bfloat16

NN = (((1,), (0,)), ((), ()))
NT = (((1,), (1,)), ((), ()))
TN = (((0,), (0,)), ((), ()))


def mm(a, b, dims=NN):
    return lax.dot_general(a, b, dims, preferred_element_type=F32)


def iota(shape, dim):
    return lax.broadcasted_iota(jnp.int32, shape, dim)


def head_sums(values, ones):
    high = values.astype(BF16)
    low = (values - high.astype(F32)).astype(BF16)
    return jnp.concatenate(
        [
            mm(high[:, g : g + LANES], ones) + mm(low[:, g : g + LANES], ones)
            for g in range(0, D, LANES)
        ],
        axis=1,
    )


def one_hot_rows(count, columns, source_of):
    return jnp.where(source_of(iota((count, 1), 0)) == iota((1, columns), 1), 1.0, 0.0).astype(BF16)


def pack_z_kernel(own_ref, cot_ref, *outs, ny, n_gy):
    inner = 4 * ny
    edge = 2 * ny
    yb = ny // n_gy
    total_z = 4 * n_gy
    window = 12 * yb
    gy = lax.axis_index("gy")
    odd = gy % 2

    def source(i):
        k = i // window
        rest = i - k * window
        px = rest // (6 * yb)
        rest = rest - px * (6 * yb)
        pz = rest // yb
        z = 4 * (gy ^ k) - 1 + pz
        return jnp.where((z >= 0) & (z < total_z), (px * yb + rest - pz * yb) * total_z + z, -1)

    win = mm(one_hot_rows(n_gy * window, 2 * yb * total_z, source), cot_ref[...]).astype(BF16)
    for k in range(n_gy):
        outs[k][0:window] = win[k * window : (k + 1) * window]
    last = 3 if n_gy == 4 else n_gy
    base = window if n_gy == 4 else 0
    for ref, start, off in ((outs[1], window, 1 - odd), (outs[last], base, odd)):
        for p in range(2):
            at = pl.multiple_of(p * inner + off * edge, edge)
            ref[start + p * edge : start + (p + 1) * edge] = own_ref[pl.ds(at, edge)]


def pack_x_kernel(own_ref, *refs, ny, n_gy):
    ins, (m1_ref, m2_ref, ext_ref, cot_ref) = refs[:-4], refs[-4:]
    inner = 4 * ny
    plane = 8 * ny
    edge = 2 * ny
    qplane = 6 * ny
    yb = ny // n_gy
    window = 12 * yb
    gx = lax.axis_index("gx")
    gy = lax.axis_index("gy")
    odd = gx % 2
    odd_z = gy % 2
    last = 3 if n_gy == 4 else n_gy
    base = window if n_gy == 4 else 0
    for p in range(2):
        ext_ref[p * plane + edge : p * plane + edge + inner] = own_ref[p * inner : (p + 1) * inner]
        for ref, start, top in ((ins[1], window, 1 - odd_z), (ins[last], base, odd_z)):
            at = pl.multiple_of(p * plane + top * qplane, edge)
            ext_ref[pl.ds(at, edge)] = ref[start + p * edge : start + (p + 1) * edge]
    got = jnp.concatenate([ins[k][0:window].astype(F32) for k in range(n_gy)], axis=0).astype(BF16)

    def source(i):
        row = i // ny
        y = i - row * ny
        src = y // yb
        return ((src ^ gy) * 12 + row) * yb + y - src * yb

    cot = mm(one_hot_rows(2 * qplane, n_gy * window, source), got).astype(BF16)
    cot_ref[0] = cot[0:qplane]
    cot_ref[1] = cot[qplane : 2 * qplane]
    for ref, p in ((m1_ref, 1 - odd), (m2_ref, odd)):
        ref[0 : 2 * plane] = ext_ref[...]
        ref[2 * plane :] = cot_ref[p]


def main_kernel(*refs, ny, n_gx, n_gy):
    ls_ref, ext_ref, m1_ref, m2_ref, cot_ref, wqkv_ref, wout_ref = refs[:7]
    pairs = n_gx // 2
    send_refs = refs[7 : 7 + pairs]
    out_ref, gin_ref, e_ref, c_ref, full_ref, bias_ref, dq_ref, dk_ref, dv_ref, att_ref = refs[7 + pairs :]
    plane = 8 * ny
    inner = 4 * ny
    qplane = 6 * ny
    edge = 2 * ny
    block = 12 * ny
    tokens = 2 * inner
    yb = ny // n_gy
    total_x, total_z = 2 * n_gx, 4 * n_gy
    gx = lax.axis_index("gx")
    gy = lax.axis_index("gy")
    odd = gx % 2
    for src, base in ((m1_ref, 4 - 4 * odd), (ext_ref, 2), (m2_ref, 4 * odd)):
        for p in range(2):
            e_ref[base + p] = src[p * plane : (p + 1) * plane]
    inside = jnp.where((gx > 0) & (gx < n_gx - 1), 1.0, 0.0)
    c_ref[1] = cot_ref[0]
    c_ref[2] = cot_ref[1]
    c_ref[3 - 3 * odd] = m1_ref[2 * plane :]
    c_ref[3 * odd] = (m2_ref[2 * plane :].astype(F32) * inside).astype(BF16)

    x = e_ref[...].reshape(6 * plane, D).astype(F32)
    r = lax.rsqrt(jnp.mean(x * x, axis=-1, keepdims=True) + EPSILON)
    normed_f = x * r
    normed = normed_f.astype(BF16)

    def query_rows(values, rows, halo):
        parts = []
        for own_plane, other in ((2, 1), (3, 4)):
            a, o = own_plane * rows - halo[0], other * rows - halo[0]
            first = halo[1]
            parts += [
                values[a + first + ny : a + first + 5 * ny],
                values[a + first : a + first + ny],
                values[a + first + 5 * ny : a + first + 6 * ny],
                values[o + first : o + first + 6 * ny],
            ]
        return jnp.concatenate(parts, axis=0)

    ones = (iota((LANES, 1), 0) // HEAD_DIM == iota((1, LANES), 1) // HEAD_DIM)
    ones = jnp.where(ones, 1.0, 0.0).astype(BF16)
    head = iota((1, D), 1) // HEAD_DIM
    scale = jnp.zeros((1, D), F32)
    for h in range(HEADS):
        scale = jnp.where(head == h, ls_ref[h] * (1.0 / HEAD_DIM), scale)

    k = mm(normed, wqkv_ref[D : 2 * D], NT)
    v = mm(normed, wqkv_ref[2 * D : 3 * D], NT)
    q = mm(query_rows(normed_f, plane, (0, ny)).astype(BF16), wqkv_ref[0:D], NT)
    rk = lax.rsqrt(head_sums(k * k, ones) * (1.0 / HEAD_DIM) + EPSILON)
    rq = lax.rsqrt(head_sums(q * q, ones) * (1.0 / HEAD_DIM) + EPSILON)
    kb = (k * rk).astype(BF16)
    vb = v.astype(BF16)
    qb = (q * rq * scale).astype(BF16)
    up = mm(c_ref[...].reshape(4 * qplane, D), wout_ref[...])
    ub = query_rows(up, qplane, (qplane, 0)).astype(BF16)

    lane = iota((1, QUAD * block), 1)
    is_own = lane < QUAD * inner
    t_own = lane % inner
    t_oth = (lane - QUAD * inner) % (8 * ny)
    in_edge = t_oth < 2 * ny
    qz = jnp.where(
        is_own,
        2 + t_own // ny,
        jnp.where(in_edge, jnp.where(t_oth < ny, 1, 6), 1 + (t_oth - 2 * ny) // ny),
    )
    qy = lane % ny
    own_plane = is_own | in_edge
    kj = iota((4 * plane, 1), 0)
    kx = kj // plane
    kr = kj - kx * plane
    kz = kr // ny
    ky = kr - kz * ny
    gz = gy * 4 - 2 + kz
    z_ok = (gz >= 0) & (gz < total_z)
    near_zy = (jnp.abs(kz - qz) <= 1) & (jnp.abs(ky - qy) <= 1)

    mask = [
        jnp.where(iota((1, LANES), 1) // HEAD_DIM == j, 1.0, 0.0).astype(BF16) for j in range(QUAD)
    ]
    for b in range(2):
        qx = jnp.where(own_plane, 2 - b, 1 + b)
        gxk = gx * 2 - 2 + 2 * b + kx
        k_ok = z_ok & (gxk >= 0) & (gxk < total_x)
        ok = near_zy & (jnp.abs(kx - qx) <= 1) & k_ok
        bias_ref[...] = jnp.where(ok, 0.0, NEGATIVE)
        first = 2 * plane if b == 0 else 0
        for g in range(0, D, LANES):
            lanes = slice(g, g + LANES)
            kq = kb[2 * b * plane : (2 * b + 4) * plane, lanes]
            vq = vb[2 * b * plane : (2 * b + 4) * plane, lanes]

            def stacked(values):
                own_part = values[b * block : b * block + inner, lanes]
                other = values[b * block + inner : (b + 1) * block, lanes]
                return jnp.concatenate(
                    [own_part * m for m in mask] + [other * m for m in mask], axis=0
                )

            qs = stacked(qb)
            us = stacked(ub)
            s = mm(kq, qs, NT) + bias_ref[...]
            w = jnp.exp(s - jnp.max(s, axis=0, keepdims=True))
            w = w * (1.0 / jnp.sum(w, axis=0, keepdims=True))
            dp = mm(vq, us, NT)
            ds = w * (dp - jnp.sum(w * dp, axis=0, keepdims=True))
            wb = w.astype(BF16)
            dsb = ds.astype(BF16)
            o_all = mm(wb[:, 0 : QUAD * inner], vq, TN)
            dq_all = mm(dsb[:, 0 : QUAD * inner], kq, TN)
            lane_head = iota((1, LANES), 1) // HEAD_DIM
            att = o_all[0:inner]
            dq = dq_all[0:inner]
            for j in range(1, QUAD):
                att = jnp.where(lane_head == j, o_all[j * inner : (j + 1) * inner], att)
                dq = jnp.where(lane_head == j, dq_all[j * inner : (j + 1) * inner], dq)
            att_ref[b * inner : (b + 1) * inner, lanes] = att
            dq_ref[b * inner : (b + 1) * inner, lanes] = dq

            def own_keys(values):
                return jnp.concatenate(
                    [values[first + p * plane + edge : first + p * plane + edge + inner] for p in range(2)],
                    axis=0,
                )

            dk = mm(own_keys(dsb), qs)
            dv = mm(own_keys(wb), us)
            if b == 0:
                dk_ref[:, lanes] = dk
                dv_ref[:, lanes] = dv
            else:
                dk_ref[:, lanes] += dk
                dv_ref[:, lanes] += dv

    def own_queries(values):
        return jnp.concatenate([values[0:inner], values[block : block + inner]], axis=0)

    def own_rows(values):
        return jnp.concatenate(
            [values[(2 + p) * plane + edge : (2 + p) * plane + edge + inner] for p in range(2)],
            axis=0,
        )

    q_o, rq_o = own_queries(q), own_queries(rq)
    cot_o = jnp.concatenate([c_ref[1 + p].astype(F32)[ny : 5 * ny] for p in range(2)], axis=0)
    k_o, rk_o, x_o, r_o = own_rows(k), own_rows(rk), own_rows(x), own_rows(r)
    dk_o = dk_ref[...]
    gq = dq_ref[...] * scale
    inv = 1.0 / HEAD_DIM
    gq_b = (rq_o * gq - q_o * (rq_o * rq_o * rq_o) * (head_sums(q_o * gq, ones) * inv)).astype(BF16)
    gk_b = (rk_o * dk_o - k_o * (rk_o * rk_o * rk_o) * (head_sums(k_o * dk_o, ones) * inv)).astype(BF16)
    gv_b = dv_ref[...].astype(BF16)
    att_b = att_ref[...].astype(BF16)
    cot_b = cot_o.astype(BF16)
    normed_b = (x_o * r_o).astype(BF16)

    width = 8 * D // n_gx
    per = D // width
    for d in range(pairs):
        part = (gq_b, gk_b, gv_b, cot_b)[d // per]
        off = (d % per) * width
        full_ref[d, :, 0:width] = part[:, off : off + width]
        full_ref[d, :, width : width + D] = normed_b if d < 3 * per else att_b
    for k in range(pairs):
        send_refs[k][...] = full_ref[(gx // 2) ^ k]

    g_norm = mm(gq_b, wqkv_ref[0:D]) + mm(gk_b, wqkv_ref[D : 2 * D]) + mm(gv_b, wqkv_ref[2 * D : 3 * D])
    g_in = r_o * g_norm - x_o * (r_o * r_o * r_o) * jnp.mean(x_o * g_norm, axis=-1, keepdims=True)
    gin = (cot_o + g_in).astype(BF16)

    def gin_source(i):
        px = i // inner
        rest = i - px * inner
        py = rest // 4
        return px * inner + (rest - py * 4) * ny + py

    gin_ref[...] = mm(one_hot_rows(tokens, tokens, gin_source), gin).astype(BF16)

    out = (x_o + mm(att_b, wout_ref[...], NT)).astype(BF16)

    def out_source(i):
        dst = i // (8 * yb)
        rest = i - dst * (8 * yb)
        px = rest // (4 * yb)
        rest = rest - px * (4 * yb)
        py = rest // 4
        return px * inner + (rest - py * 4) * ny + dst * yb + py

    moved = mm(one_hot_rows(tokens, tokens, out_source), out).astype(BF16)
    for d in range(n_gy):
        out_ref[d] = moved[d * 8 * yb : (d + 1) * 8 * yb]


def partial_kernel(*refs):
    ins, (mine_ref, other_ref, both_ref) = refs[:-3], refs[-3:]
    width = mine_ref.shape[0]
    left = jnp.concatenate([ref[:, 0 : 2 * width] for ref in ins], axis=0)
    right = jnp.concatenate([ref[:, 2 * width :] for ref in ins], axis=0)
    partial = mm(left, right, TN)
    both_ref[0] = partial[0:width]
    both_ref[1] = partial[width:]
    odd = lax.axis_index("gx") % 2
    mine_ref[...] = both_ref[odd]
    other_ref[...] = both_ref[1 - odd].astype(BF16)


def scatter_kernel(mine_ref, other_ref, out_ref, keep_ref, *refs, n_gy):
    sends, sum_ref = refs[:-1], refs[-1]
    rows, extra = keep_ref.shape[0], out_ref.shape[1]
    total = mine_ref[...] + other_ref[...].astype(F32)
    for d in range(n_gy):
        sum_ref[d] = total[d * rows : (d + 1) * rows]
    gy = lax.axis_index("gy")
    keep_ref[...] = sum_ref[gy]
    for k in range(1, n_gy):
        sends[k - 1][0:rows] = sum_ref[gy ^ k].astype(BF16)
        sends[k - 1][rows : rows + extra] = out_ref[gy ^ k]


def final_kernel(keep_ref, own_ref, *refs, n_gy, factor):
    ins, (gw_ref, out_ref, got_ref) = refs[:-3], refs[-3:]
    rows, extra = keep_ref.shape[0], own_ref.shape[1]
    gy = lax.axis_index("gy")
    total = keep_ref[...]
    got_ref[gy] = own_ref[gy]
    for k in range(1, n_gy):
        total = total + ins[k - 1][0:rows].astype(F32)
        got_ref[gy ^ k] = ins[k - 1][rows : rows + extra]
    gw_ref[...] = total * factor

    def source(i):
        xy = i // (4 * n_gy)
        rest = i - xy * (4 * n_gy)
        src = rest // 4
        return src * extra + xy * 4 + rest - src * 4

    got = got_ref[...].reshape(n_gy * extra, D)
    out_ref[...] = mm(one_hot_rows(n_gy * extra, n_gy * extra, source), got).astype(BF16)


def matchings(count):
    first = [(i, i ^ 1) for i in range(count)]
    second = [((i - 1) % count, i) for i in range(0, count, 2)]
    second += [(t, s) for s, t in second]
    return first, second


def call(kernel, name, args, outs, scratch=(), smem=0, results=0, limit=8):
    vmem = pl.BlockSpec(memory_space=pltpu.VMEM)
    args = list(args[:smem]) + [
        pltpu.with_memory_space_constraint(a, pltpu.VMEM) for a in args[smem:]
    ]
    inner = len(outs) - results
    return pl.pallas_call(
        kernel,
        name=name,
        out_shape=tuple(
            pltpu.VMEM(s, t) if i < inner else jax.ShapeDtypeStruct(s, t)
            for i, (s, t) in enumerate(outs)
        ),
        in_specs=[pl.BlockSpec(memory_space=pltpu.SMEM)] * smem + [vmem] * (len(args) - smem),
        out_specs=(vmem,) * len(outs),
        scratch_shapes=[pltpu.VMEM(s, t) for s, t in scratch],
        compiler_params=pltpu.CompilerParams(vmem_limit_bytes=limit << 20),
    )(*args)


def on_device(slab_tokens, cotangent, w_qkv, w_out, logit_scale):
    size_x, ny, size_z, _ = slab_tokens.shape
    n_gx = lax.axis_size("gx")
    n_gy = lax.axis_size("gy")
    yb = cotangent.shape[1]
    total_x, total_z = size_x * n_gx, size_z * n_gy
    assert size_x == 2 and size_z == 4 and cotangent.shape[0] == 2
    assert cotangent.shape[2] == total_z and yb * n_gy == ny
    tokens = size_x * ny * size_z
    gx1, gx2 = matchings(n_gx)
    gy1, gy2 = matchings(n_gy)

    def swapped(value, axis, k):
        count = lax.axis_size(axis)
        return lax.ppermute(value, axis, [(i, i ^ k) for i in range(count)])

    own = jnp.transpose(slab_tokens, (0, 2, 1, 3)).reshape(tokens, D)
    cot = cotangent.reshape(2 * yb * total_z, D)
    window, edges = 12 * yb, 4 * ny
    merged = n_gy == 4
    sizes = [window + (edges if k == 1 or (merged and k == 3) else 0) for k in range(n_gy)]
    if not merged:
        sizes.append(edges)
    packed = call(
        lambda *refs: pack_z_kernel(*refs, ny=ny, n_gy=n_gy),
        "pack_z",
        (own, cot),
        [((s, D), BF16) for s in sizes],
    )
    order = [1] + ([3, 2] if merged else list(range(2, n_gy)))
    moved = {0: packed[0]}
    for k in order:
        moved[k] = swapped(packed[k], "gy", k)
    if not merged:
        moved[n_gy] = lax.ppermute(packed[n_gy], "gy", gy2)
    x_payload = ((16 * ny + 6 * ny, D), BF16)
    p1, p2, ext, cot_own = call(
        lambda *refs: pack_x_kernel(*refs, ny=ny, n_gy=n_gy),
        "pack_x",
        (own,) + tuple(moved[k] for k in range(len(sizes))),
        (x_payload, x_payload, ((16 * ny, D), BF16), ((2, 6 * ny, D), BF16)),
    )
    m1 = lax.ppermute(p1, "gx", gx1)
    m2 = lax.ppermute(p2, "gx", gx2)

    width = 4 * D // n_gx
    pairs = n_gx // 2
    extra = tokens // n_gy
    rows = width // n_gy
    results = call(
        lambda *refs: main_kernel(*refs, ny=ny, n_gx=n_gx, n_gy=n_gy),
        "layer",
        (logit_scale, ext, m1, m2, cot_own, w_qkv, w_out),
        [((tokens, 2 * width + D), BF16)] * pairs
        + [((n_gy, extra, D), BF16), ((tokens, D), BF16)],
        scratch=(
            ((6, 8 * ny, D), BF16),
            ((4, 6 * ny, D), BF16),
            ((pairs, tokens, 2 * width + D), BF16),
            ((32 * ny, QUAD * 12 * ny), F32),
            ((tokens, D), F32),
            ((tokens, D), F32),
            ((tokens, D), F32),
            ((tokens, D), F32),
        ),
        smem=1,
        limit=24,
    )
    sends, out_rows, gin = results[:pairs], results[pairs], results[pairs + 1]
    arrived = [sends[0]] + [swapped(sends[k], "gx", 2 * k) for k in range(1, pairs)]
    mine, other = call(
        partial_kernel,
        "partial",
        arrived,
        (((width, D), F32), ((width, D), BF16)),
        scratch=(((2, width, D), F32),),
        limit=12,
    )
    other = swapped(other, "gx", 1)
    keep, *blocks = call(
        lambda *refs: scatter_kernel(*refs, n_gy=n_gy),
        "scatter",
        (mine, other, out_rows),
        [((rows, D), F32)] + [((rows + extra, D), BF16)] * (n_gy - 1),
        scratch=(((n_gy, rows, D), F32),),
    )
    blocks = [swapped(blocks[k - 1], "gy", k) for k in range(1, n_gy)]
    factor = 1.0 / math.sqrt(total_x * ny * total_z)
    grad_weights, output = call(
        lambda *refs: final_kernel(*refs, n_gy=n_gy, factor=factor),
        "final",
        [keep, out_rows] + blocks,
        (((rows, D), F32), ((n_gy * extra, D), BF16)),
        scratch=(((n_gy, extra, D), BF16),),
        results=2,
    )
    return (
        output.reshape(2, yb, total_z, D),
        gin.reshape(2, ny, 4, D),
        grad_weights,
    )


def solution(mesh):
    return jax.shard_map(
        on_device,
        mesh=mesh,
        in_specs=(P("gx", None, "gy", None), P("gx", "gy", None, None), P(), P(), P()),
        out_specs=(P("gx", "gy", None, None), P("gx", None, "gy", None), P(("gx", "gy"), None)),
        check_vma=False,
    )
```

```python
import math

import jax
import jax.numpy as jnp
from jax import lax
from jax.experimental import pallas as pl
from jax.experimental.pallas import tpu as pltpu
from jax.sharding import PartitionSpec as P

D = 512
HEADS = 8
HEAD_DIM = 64
QUAD = 4
LANES = QUAD * HEAD_DIM
EPSILON = 1e-06
NEGATIVE = -1e30
F32 = jnp.float32
BF16 = jnp.bfloat16

NN = (((1,), (0,)), ((), ()))
NT = (((1,), (1,)), ((), ()))
TN = (((0,), (0,)), ((), ()))


def mm(a, b, dims=NN):
    return lax.dot_general(a, b, dims, preferred_element_type=F32)


def iota(shape, dim):
    return lax.broadcasted_iota(jnp.int32, shape, dim)


def head_sums(values, ones):
    high = values.astype(BF16)
    low = (values - high.astype(F32)).astype(BF16)
    return jnp.concatenate(
        [
            mm(high[:, g : g + LANES], ones) + mm(low[:, g : g + LANES], ones)
            for g in range(0, D, LANES)
        ],
        axis=1,
    )


def one_hot_rows(count, columns, source_of):
    return jnp.where(source_of(iota((count, 1), 0)) == iota((1, columns), 1), 1.0, 0.0).astype(BF16)


def pack_z_kernel(slab_hbm, cot_hbm, own_ref, *refs, ny, n_gy):
    inner = 4 * ny
    edge = 2 * ny
    yb = ny // n_gy
    total_z = 4 * n_gy
    window = 12 * yb
    gy = lax.axis_index("gy")
    odd = gy % 2
    outs, (slab_ref, cot_ref, sem_ref) = refs[:-3], refs[-3:]
    slab_copy = pltpu.make_async_copy(slab_hbm, slab_ref, sem_ref.at[0])
    cot_copy = pltpu.make_async_copy(cot_hbm, cot_ref, sem_ref.at[1])
    slab_copy.start()
    cot_copy.start()

    def own_source(i):
        row = i // ny
        px = row // 4
        return (px * ny + i - row * ny) * 4 + row - px * 4

    def source(i):
        k = i // window
        rest = i - k * window
        px = rest // (6 * yb)
        rest = rest - px * (6 * yb)
        pz = rest // yb
        z = 4 * (gy ^ k) - 1 + pz
        return jnp.where((z >= 0) & (z < total_z), (px * yb + rest - pz * yb) * total_z + z, -1)

    moves = one_hot_rows(2 * inner, 2 * inner, own_source)
    windows = one_hot_rows(n_gy * window, 2 * yb * total_z, source)
    slab_copy.wait()
    rows = jnp.concatenate(
        [slab_ref[p, y].astype(F32) for p in range(2) for y in range(ny)], axis=0
    )
    own_ref[...] = mm(moves, rows.astype(BF16)).astype(BF16)
    cot_copy.wait()
    win = mm(windows, cot_ref[...]).astype(BF16)
    for k in range(n_gy):
        outs[k][0:window] = win[k * window : (k + 1) * window]
    last = 3 if n_gy == 4 else n_gy
    base = window if n_gy == 4 else 0
    for ref, start, off in ((outs[1], window, 1 - odd), (outs[last], base, odd)):
        for p in range(2):
            at = pl.multiple_of(p * inner + off * edge, edge)
            ref[start + p * edge : start + (p + 1) * edge] = own_ref[pl.ds(at, edge)]


def pack_x_kernel(own_ref, *refs, ny, n_gy):
    ins, (m1_ref, m2_ref, ext_ref, cot_ref) = refs[:-4], refs[-4:]
    inner = 4 * ny
    plane = 8 * ny
    edge = 2 * ny
    qplane = 6 * ny
    yb = ny // n_gy
    window = 12 * yb
    gx = lax.axis_index("gx")
    gy = lax.axis_index("gy")
    odd = gx % 2
    odd_z = gy % 2
    last = 3 if n_gy == 4 else n_gy
    base = window if n_gy == 4 else 0
    for p in range(2):
        ext_ref[p * plane + edge : p * plane + edge + inner] = own_ref[p * inner : (p + 1) * inner]
        for ref, start, top in ((ins[1], window, 1 - odd_z), (ins[last], base, odd_z)):
            at = pl.multiple_of(p * plane + top * qplane, edge)
            ext_ref[pl.ds(at, edge)] = ref[start + p * edge : start + (p + 1) * edge]
    got = jnp.concatenate([ins[k][0:window].astype(F32) for k in range(n_gy)], axis=0).astype(BF16)

    def source(i):
        row = i // ny
        y = i - row * ny
        src = y // yb
        return ((src ^ gy) * 12 + row) * yb + y - src * yb

    cot = mm(one_hot_rows(2 * qplane, n_gy * window, source), got).astype(BF16)
    cot_ref[0] = cot[0:qplane]
    cot_ref[1] = cot[qplane : 2 * qplane]
    for ref, p in ((m1_ref, 1 - odd), (m2_ref, odd)):
        ref[0 : 2 * plane] = ext_ref[...]
        ref[2 * plane :] = cot_ref[p]


def rms_scale(x):
    return lax.rsqrt(jnp.mean(x * x, axis=-1, keepdims=True) + EPSILON)


def head_ones():
    same = iota((LANES, 1), 0) // HEAD_DIM == iota((1, LANES), 1) // HEAD_DIM
    return jnp.where(same, 1.0, 0.0).astype(BF16)


def head_scale(values, ones):
    return lax.rsqrt(head_sums(values * values, ones) * (1.0 / HEAD_DIM) + EPSILON)


def head_back(values, scale, grad, ones):
    mean = head_sums(values * grad, ones) * (1.0 / HEAD_DIM)
    return (scale * grad - values * (scale * scale * scale) * mean).astype(BF16)


def side_queries(n_ref, own_cot, side_cot, high, ny):
    own, side = n_ref[2 + high], n_ref[1 - high]
    rows = jnp.concatenate(
        [own[2 * ny : 6 * ny], own[ny : 2 * ny], own[6 * ny : 7 * ny], side[ny : 7 * ny]], axis=0
    )
    cots = jnp.concatenate(
        [own_cot[ny : 5 * ny], own_cot[0:ny], own_cot[5 * ny : 6 * ny], side_cot], axis=0
    )
    return rows.astype(BF16), cots.astype(BF16)


def side_attention(
    scale, q, ub, kb, vb, high, ones, bias_ref, gq_ref, att_ref, dq_ref, dk_ref, dv_ref,
    *, ny, n_gx, n_gy,
):
    plane = 8 * ny
    inner = 4 * ny
    edge = 2 * ny
    block = 12 * ny
    total_x, total_z = 2 * n_gx, 4 * n_gy
    gx = lax.axis_index("gx")
    gy = lax.axis_index("gy")
    rq = head_scale(q, ones)
    qb = (q * rq * scale).astype(BF16)

    lane = iota((1, QUAD * block), 1)
    is_own = lane < QUAD * inner
    t_own = lane % inner
    t_oth = (lane - QUAD * inner) % (8 * ny)
    in_edge = t_oth < 2 * ny
    qz = jnp.where(
        is_own,
        2 + t_own // ny,
        jnp.where(in_edge, jnp.where(t_oth < ny, 1, 6), 1 + (t_oth - 2 * ny) // ny),
    )
    qy = lane % ny
    qx = jnp.where(is_own | in_edge, high, 3 * high - 1)
    kj = iota((4 * plane, 1), 0)
    kp = kj // plane
    kr = kj - kp * plane
    kz = kr // ny
    ky = kr - kz * ny
    kx = jnp.where(kp < 2, kp + 4 * high - 2, kp - 2)
    gz = gy * 4 - 2 + kz
    gxk = gx * 2 + kx
    k_ok = (gz >= 0) & (gz < total_z) & (gxk >= 0) & (gxk < total_x)
    ok = (jnp.abs(kz - qz) <= 1) & (jnp.abs(ky - qy) <= 1) & (jnp.abs(kx - qx) <= 1) & k_ok
    bias_ref[...] = jnp.where(ok, 0.0, NEGATIVE)

    lane_head = iota((1, LANES), 1) // HEAD_DIM
    mask = [jnp.where(lane_head == j, 1.0, 0.0).astype(BF16) for j in range(QUAD)]

    def own_keys(values):
        return jnp.concatenate(
            [values[(2 + p) * plane + edge : (2 + p) * plane + edge + inner] for p in range(2)],
            axis=0,
        )

    for g in range(0, D, LANES):
        lanes = slice(g, g + LANES)
        kq, vq = kb[:, lanes], vb[:, lanes]

        def stacked(values):
            return jnp.concatenate(
                [values[0:inner, lanes] * m for m in mask]
                + [values[inner:block, lanes] * m for m in mask],
                axis=0,
            )

        qs = stacked(qb)
        us = stacked(ub)
        s = mm(kq, qs, NT) + bias_ref[...]
        w = jnp.exp(s - jnp.max(s, axis=0, keepdims=True))
        w = w * (1.0 / jnp.sum(w, axis=0, keepdims=True))
        dp = mm(vq, us, NT)
        ds = w * (dp - jnp.sum(w * dp, axis=0, keepdims=True))
        wb = w.astype(BF16)
        dsb = ds.astype(BF16)
        o_all = mm(wb[:, 0 : QUAD * inner], vq, TN)
        dq_all = mm(dsb[:, 0 : QUAD * inner], kq, TN)
        att = o_all[0:inner]
        dq = dq_all[0:inner]
        for j in range(1, QUAD):
            att = jnp.where(lane_head == j, o_all[j * inner : (j + 1) * inner], att)
            dq = jnp.where(lane_head == j, dq_all[j * inner : (j + 1) * inner], dq)
        att_ref[:, lanes] = att.astype(BF16)
        dq_ref[:, lanes] = dq
        dk_ref[:, lanes] = mm(own_keys(dsb), qs)
        dv_ref[:, lanes] = mm(own_keys(wb), us)
    gq_ref[...] = head_back(q[0:inner], rq[0:inner], dq_ref[...] * scale, ones)


def near_kernel(
    ext_ref, m_ref, cot_ref, wqkv_hbm, wout_hbm, ls_hbm,
    wqkv_ref, wout_ref, scale_ref, kb_ref, vb_ref, k_ref, rk_ref, gq_ref, att_ref, dk_ref, dv_ref,
    n_ref, bias_ref, dq_ref, ls_ref, sem_ref,
    *, ny, n_gx, n_gy,
):
    copies = [
        pltpu.make_async_copy(wqkv_hbm.at[pl.ds(i * D, D)], wqkv_ref.at[pl.ds(i * D, D)], sem_ref.at[i])
        for i in range(3)
    ]
    copies.append(pltpu.make_async_copy(wout_hbm, wout_ref, sem_ref.at[3]))
    copies.append(pltpu.make_async_copy(ls_hbm, ls_ref, sem_ref.at[4]))
    for i in (1, 2, 0, 3, 4):
        copies[i].start()
    plane = 8 * ny
    high = 1 - lax.axis_index("gx") % 2
    for i, src in enumerate((m_ref, ext_ref)):
        x = src[0 : 2 * plane].astype(F32)
        n = x * rms_scale(x)
        n_ref[2 * i] = n[0:plane]
        n_ref[2 * i + 1] = n[plane:]
    ones = head_ones()
    normed = n_ref[...].reshape(4 * plane, D).astype(BF16)
    copies[1].wait()
    k = mm(normed, wqkv_ref[D : 2 * D], NT)
    rk = head_scale(k, ones)
    kb = (k * rk).astype(BF16)
    copies[2].wait()
    vb = mm(normed, wqkv_ref[2 * D : 3 * D], NT).astype(BF16)
    kb_ref[...] = kb[2 * plane :]
    vb_ref[...] = vb[2 * plane :]
    for p in range(2):
        at = (2 + p) * plane + 2 * ny
        k_ref[p * 4 * ny : (p + 1) * 4 * ny] = k[at : at + 4 * ny]
        rk_ref[p * 4 * ny : (p + 1) * 4 * ny] = rk[at : at + 4 * ny]
    side_cot = m_ref[2 * plane :].astype(F32)
    rows, cots = side_queries(n_ref, cot_ref[high].astype(F32), side_cot, high, ny)
    copies[0].wait()
    q = mm(rows, wqkv_ref[0:D], NT)
    copies[3].wait()
    copies[4].wait()
    head = iota((1, D), 1) // HEAD_DIM
    scale = jnp.zeros((1, D), F32)
    for h in range(HEADS):
        scale = jnp.where(head == h, ls_ref[h] * (1.0 / HEAD_DIM), scale)
    scale_ref[...] = scale
    ub = mm(cots, wout_ref[...]).astype(BF16)
    side_attention(
        scale, q, ub, kb, vb, high, ones, bias_ref, gq_ref, att_ref, dq_ref, dk_ref, dv_ref,
        ny=ny, n_gx=n_gx, n_gy=n_gy,
    )


def far_kernel(*refs, ny, n_gx, n_gy):
    pairs = n_gx // 2
    ext_ref, m_ref, cot_ref, wqkv_ref, wout_ref, scale_ref, kb_ref, vb_ref, k_ref, rk_ref = refs[:10]
    scale = scale_ref[...]
    gq1_ref, att1_ref, dk1_ref, dv1_ref = refs[10:14]
    send_refs = refs[14 : 14 + pairs]
    g_ref, a_ref = refs[14 + pairs : 16 + pairs]
    n_ref, bias_ref, dq_ref, gq_ref, att_ref, dk_ref, dv_ref, full_ref, b_ref = refs[16 + pairs :]
    plane = 8 * ny
    inner = 4 * ny
    gx = lax.axis_index("gx")
    high = gx % 2
    for i, src in enumerate((m_ref, ext_ref)):
        x = src[0 : 2 * plane].astype(F32)
        n = x * rms_scale(x)
        n_ref[2 * i] = n[0:plane]
        n_ref[2 * i + 1] = n[plane:]
    ones = head_ones()
    normed = n_ref[0:2].reshape(2 * plane, D).astype(BF16)
    k = mm(normed, wqkv_ref[D : 2 * D], NT)
    kb = jnp.concatenate([(k * head_scale(k, ones)).astype(BF16), kb_ref[...]], axis=0)
    v = mm(normed, wqkv_ref[2 * D : 3 * D], NT)
    vb = jnp.concatenate([v.astype(BF16), vb_ref[...]], axis=0)
    inside = jnp.where((gx > 0) & (gx < n_gx - 1), 1.0, 0.0)
    side_cot = m_ref[2 * plane :].astype(F32) * inside
    rows, cots = side_queries(n_ref, cot_ref[high].astype(F32), side_cot, high, ny)
    q = mm(rows, wqkv_ref[0:D], NT)
    ub = mm(cots, wout_ref[...]).astype(BF16)
    side_attention(
        scale, q, ub, kb, vb, high, ones, bias_ref, gq_ref, att_ref, dq_ref, dk_ref, dv_ref,
        ny=ny, n_gx=n_gx, n_gy=n_gy,
    )
    dk = dk1_ref[...] + dk_ref[...]
    gk_b = head_back(k_ref[...], rk_ref[...], dk, ones)
    gv_b = (dv1_ref[...] + dv_ref[...]).astype(BF16)
    b_ref[0, 1 - high] = gq1_ref[...]
    b_ref[0, high] = gq_ref[...]
    b_ref[1, 1 - high] = att1_ref[...]
    b_ref[1, high] = att_ref[...]
    gq_b = b_ref[0].reshape(2 * inner, D)
    att_b = b_ref[1].reshape(2 * inner, D)
    cot_b = jnp.concatenate(
        [cot_ref[p].astype(F32)[ny : 5 * ny] for p in range(2)], axis=0
    ).astype(BF16)
    normed_b = jnp.concatenate([n_ref[2 + p][2 * ny : 6 * ny] for p in range(2)], axis=0).astype(BF16)

    width = 8 * D // n_gx
    per = D // width
    for d in range(pairs):
        part = (gq_b, gk_b, gv_b, cot_b)[d // per]
        off = (d % per) * width
        full_ref[d, :, 0:width] = part[:, off : off + width]
        full_ref[d, :, width : width + D] = normed_b if d < 3 * per else att_b
    for k in range(pairs):
        send_refs[k][...] = full_ref[(gx // 2) ^ k]
    for i, part in enumerate((gq_b, gk_b, gv_b)):
        g_ref[i] = part
    a_ref[...] = att_b


def token_kernel(ext_ref, cot_ref, g_ref, a_ref, wqkv_ref, wout_ref, out_ref, gin_ref, *, ny, n_gy):
    plane = 8 * ny
    inner = 4 * ny
    tokens = 2 * inner
    yb = ny // n_gy
    x = jnp.concatenate(
        [ext_ref[p * plane + 2 * ny : p * plane + 6 * ny].astype(F32) for p in range(2)], axis=0
    )
    r = rms_scale(x)
    cot = jnp.concatenate([cot_ref[p].astype(F32)[ny : 5 * ny] for p in range(2)], axis=0)
    g_norm = mm(g_ref[0], wqkv_ref[0:D])
    for i in range(1, 3):
        g_norm = g_norm + mm(g_ref[i], wqkv_ref[i * D : (i + 1) * D])
    g_in = r * g_norm - x * (r * r * r) * jnp.mean(x * g_norm, axis=-1, keepdims=True)
    gin = (cot + g_in).astype(BF16)

    def gin_source(i):
        px = i // inner
        rest = i - px * inner
        py = rest // 4
        return px * inner + (rest - py * 4) * ny + py

    gin_ref[...] = mm(one_hot_rows(tokens, tokens, gin_source), gin).astype(BF16)

    out = (x + mm(a_ref[...], wout_ref[...], NT)).astype(BF16)

    def out_source(i):
        dst = i // (8 * yb)
        rest = i - dst * (8 * yb)
        px = rest // (4 * yb)
        rest = rest - px * (4 * yb)
        py = rest // 4
        return px * inner + (rest - py * 4) * ny + dst * yb + py

    moved = mm(one_hot_rows(tokens, tokens, out_source), out).astype(BF16)
    for d in range(n_gy):
        out_ref[d] = moved[d * 8 * yb : (d + 1) * 8 * yb]


def partial_kernel(*refs):
    ins, (mine_ref, other_ref, both_ref) = refs[:-3], refs[-3:]
    width = mine_ref.shape[0]
    left = jnp.concatenate([ref[:, 0 : 2 * width] for ref in ins], axis=0)
    right = jnp.concatenate([ref[:, 2 * width :] for ref in ins], axis=0)
    partial = mm(left, right, TN)
    both_ref[0] = partial[0:width]
    both_ref[1] = partial[width:]
    odd = lax.axis_index("gx") % 2
    mine_ref[...] = both_ref[odd]
    other_ref[...] = both_ref[1 - odd].astype(BF16)


def scatter_kernel(mine_ref, other_ref, out_ref, keep_ref, *refs, n_gy):
    sends, sum_ref = refs[:-1], refs[-1]
    rows, extra = keep_ref.shape[0], out_ref.shape[1]
    total = mine_ref[...] + other_ref[...].astype(F32)
    for d in range(n_gy):
        sum_ref[d] = total[d * rows : (d + 1) * rows]
    gy = lax.axis_index("gy")
    keep_ref[...] = sum_ref[gy]
    for k in range(1, n_gy):
        sends[k - 1][0:rows] = sum_ref[gy ^ k].astype(BF16)
        sends[k - 1][rows : rows + extra] = out_ref[gy ^ k]


def final_kernel(keep_ref, own_ref, *refs, n_gy, factor):
    ins, (gw_ref, out_ref, got_ref) = refs[:-3], refs[-3:]
    rows, extra = keep_ref.shape[0], own_ref.shape[1]
    gy = lax.axis_index("gy")
    total = keep_ref[...]
    got_ref[gy] = own_ref[gy]
    for k in range(1, n_gy):
        total = total + ins[k - 1][0:rows].astype(F32)
        got_ref[gy ^ k] = ins[k - 1][rows : rows + extra]
    gw_ref[...] = total * factor

    def source(i):
        xy = i // (4 * n_gy)
        rest = i - xy * (4 * n_gy)
        src = rest // 4
        return src * extra + xy * 4 + rest - src * 4

    got = got_ref[...].reshape(n_gy * extra, D)
    out_ref[...] = mm(one_hot_rows(n_gy * extra, n_gy * extra, source), got).astype(BF16)


def matchings(count):
    first = [(i, i ^ 1) for i in range(count)]
    second = [((i - 1) % count, i) for i in range(0, count, 2)]
    second += [(t, s) for s, t in second]
    return first, second


def call(
    kernel, name, args, outs, scratch=(), scalars=0, semaphores=0, outside=0, results=0, limit=8
):
    vmem = pl.BlockSpec(memory_space=pltpu.VMEM)
    inner = len(args) - outside
    args = list(args)
    for i in range(len(args)):
        space = pltpu.VMEM if i < inner else pltpu.HBM
        args[i] = pltpu.with_memory_space_constraint(args[i], space)
    kept = len(outs) - results
    scratches = [pltpu.VMEM(s, t) for s, t in scratch]
    if scalars:
        scratches.append(pltpu.SMEM((scalars,), F32))
    if semaphores:
        scratches.append(pltpu.SemaphoreType.DMA((semaphores,)))
    return pl.pallas_call(
        kernel,
        name=name,
        out_shape=tuple(
            pltpu.VMEM(s, t) if i < kept else jax.ShapeDtypeStruct(s, t)
            for i, (s, t) in enumerate(outs)
        ),
        in_specs=[vmem] * inner
        + [pl.BlockSpec(memory_space=pltpu.HBM)] * outside,
        out_specs=(vmem,) * len(outs),
        scratch_shapes=scratches,
        compiler_params=pltpu.CompilerParams(vmem_limit_bytes=limit << 20),
    )(*args)


def on_device(slab_tokens, cotangent, w_qkv, w_out, logit_scale):
    size_x, ny, size_z, _ = slab_tokens.shape
    n_gx = lax.axis_size("gx")
    n_gy = lax.axis_size("gy")
    yb = cotangent.shape[1]
    total_x, total_z = size_x * n_gx, size_z * n_gy
    assert size_x == 2 and size_z == 4 and cotangent.shape[0] == 2
    assert cotangent.shape[2] == total_z and yb * n_gy == ny
    tokens = size_x * ny * size_z
    gx1, gx2 = matchings(n_gx)
    gy1, gy2 = matchings(n_gy)

    def swapped(value, axis, k):
        count = lax.axis_size(axis)
        return lax.ppermute(value, axis, [(i, i ^ k) for i in range(count)])

    cot = cotangent.reshape(2 * yb * total_z, D)
    window, edges = 12 * yb, 4 * ny
    merged = n_gy == 4
    sizes = [window + (edges if k == 1 or (merged and k == 3) else 0) for k in range(n_gy)]
    if not merged:
        sizes.append(edges)
    own, *packed = call(
        lambda *refs: pack_z_kernel(*refs, ny=ny, n_gy=n_gy),
        "pack_z",
        (slab_tokens, cot),
        [((tokens, D), BF16)] + [((s, D), BF16) for s in sizes],
        scratch=(((2, ny, 4, D), BF16), ((2 * yb * total_z, D), BF16)),
        semaphores=2,
        outside=2,
    )
    order = [1] + ([3, 2] if merged else list(range(2, n_gy)))
    moved = {0: packed[0]}
    for k in order:
        moved[k] = swapped(packed[k], "gy", k)
    if not merged:
        moved[n_gy] = lax.ppermute(packed[n_gy], "gy", gy2)
    x_payload = ((16 * ny + 6 * ny, D), BF16)
    p1, p2, ext, cot_own = call(
        lambda *refs: pack_x_kernel(*refs, ny=ny, n_gy=n_gy),
        "pack_x",
        (own,) + tuple(moved[k] for k in range(len(sizes))),
        (x_payload, x_payload, ((16 * ny, D), BF16), ((2, 6 * ny, D), BF16)),
    )
    m1 = lax.ppermute(p1, "gx", gx1)
    m2 = lax.ppermute(p2, "gx", gx2)

    width = 4 * D // n_gx
    pairs = n_gx // 2
    extra = tokens // n_gy
    rows = width // n_gy
    dims = dict(ny=ny, n_gx=n_gx, n_gy=n_gy)
    half = tokens // 2
    near = call(
        lambda *refs: near_kernel(*refs, **dims),
        "near",
        (ext, m1, cot_own, w_qkv, w_out, logit_scale),
        (
            ((3 * D, D), BF16),
            ((D, D), BF16),
            ((1, D), F32),
            ((16 * ny, D), BF16),
            ((16 * ny, D), BF16),
            ((tokens, D), F32),
            ((tokens, D), F32),
            ((half, D), BF16),
            ((half, D), BF16),
            ((tokens, D), F32),
            ((tokens, D), F32),
        ),
        scratch=(
            ((4, 8 * ny, D), F32),
            ((32 * ny, QUAD * 12 * ny), F32),
            ((half, D), F32),
        ),
        scalars=HEADS,
        semaphores=5,
        outside=3,
        limit=24,
    )
    wq, wo = near[:2]
    *sends, grads, att = call(
        lambda *refs: far_kernel(*refs, **dims),
        "far",
        (ext, m2, cot_own, wq, wo) + tuple(near[2:]),
        [((tokens, 2 * width + D), BF16)] * pairs + [((3, tokens, D), BF16), ((tokens, D), BF16)],
        scratch=(
            ((4, 8 * ny, D), F32),
            ((32 * ny, QUAD * 12 * ny), F32),
            ((half, D), F32),
            ((half, D), BF16),
            ((half, D), BF16),
            ((tokens, D), F32),
            ((tokens, D), F32),
            ((pairs, tokens, 2 * width + D), BF16),
            ((2, 2, half, D), BF16),
        ),
        limit=24,
    )
    out_rows, gin = call(
        lambda *refs: token_kernel(*refs, ny=ny, n_gy=n_gy),
        "token",
        (ext, cot_own, grads, att, wq, wo),
        (((n_gy, extra, D), BF16), ((tokens, D), BF16)),
    )
    arrived = [sends[0]] + [swapped(sends[k], "gx", 2 * k) for k in range(1, pairs)]
    mine, other = call(
        partial_kernel,
        "partial",
        arrived,
        (((width, D), F32), ((width, D), BF16)),
        scratch=(((2, width, D), F32),),
        limit=12,
    )
    other = swapped(other, "gx", 1)
    keep, *blocks = call(
        lambda *refs: scatter_kernel(*refs, n_gy=n_gy),
        "scatter",
        (mine, other, out_rows),
        [((rows, D), F32)] + [((rows + extra, D), BF16)] * (n_gy - 1),
        scratch=(((n_gy, rows, D), F32),),
    )
    blocks = [swapped(blocks[k - 1], "gy", k) for k in range(1, n_gy)]
    factor = 1.0 / math.sqrt(total_x * ny * total_z)
    grad_weights, output = call(
        lambda *refs: final_kernel(*refs, n_gy=n_gy, factor=factor),
        "final",
        [keep, out_rows] + blocks,
        (((rows, D), F32), ((n_gy * extra, D), BF16)),
        scratch=(((n_gy, extra, D), BF16),),
        results=2,
    )
    return (
        output.reshape(2, yb, total_z, D),
        gin.reshape(2, ny, 4, D),
        grad_weights,
    )


def solution(mesh):
    return jax.shard_map(
        on_device,
        mesh=mesh,
        in_specs=(P("gx", None, "gy", None), P("gx", "gy", None, None), P(), P(), P()),
        out_specs=(P("gx", "gy", None, None), P("gx", None, "gy", None), P(("gx", "gy"), None)),
        check_vma=False,
    )
```
